512 devices in a mesh: gx: 32 (over y, x), gy: 16 (over z, core).
Axes of the slice: x: 4, y: 8, z: 8, core: 2. Of those that a mesh axis runs over, the one named last changes fastest.
Arguments:
- diag_blocks: float32 [9, 2048, 2048], P(None, 'gx', 'gy'), may hold values from 0 to 36, as said below
- edge_blocks: float32 [4, 9, 2048, 2048], P(None, None, 'gx', 'gy'), may hold values from -0.3 to 0.3
- edge_mask: int32 [4, 2048, 2048], P(None, 'gx', 'gy'), may hold values 0 or 1
- src_values: float32 [3, 524288], P(None, ('gx', 'gy')), may hold values from -48 to 48
- src_owner: int32 [524288, 1], P(('gx', 'gy')), may hold values from 0 to 31; in each aligned block of 1024 rows (0 to 1023, 1024 to 2047, ...) at most 64 rows name the same one
- src_node: int32 [524288], P(('gx', 'gy')), may hold values from 0 to 8191
- src_count: int32 [512], P(('gx', 'gy')), may hold values from 256 to 1024, as said below
- surf_node: int32 [1048576], P(('gx', 'gy')), may hold values from 0 to 8191
- surf_param: float32 [3, 1048576], P(None, ('gx', 'gy')), may hold values from 0 to 1
- tile_box: int32 [8192], P(('gx', 'gy')), may hold values from 0 to 511
Outputs:
- adjoint_field: float32 [3, 2048, 2048], P(None, 'gx', 'gy')
- box_gradient: float32 [512, 192], P(('gx', 'gy'))
The draws below stay inside these ranges and needn't reach their ends.
Inputs may be any that keep to these rules, and one draw needn't show every extreme that they name: `src_owner`: each device's rows name every gx index at most 64 times. `src_count`: some device has all 1024 rows live. `diag_blocks`: entries 0, 4 and 8 lie between 6 and 36; the other entries between 0 and 1.
All inputs are finite; a program needn't handle non-finite values. No bound on the sum of `edge_mask` on one device may be relied on, other than what follows from the above.
Results may differ from the reference program's by a relative error of at most 0.0015.
Values sent between devices are 32-bit elements; how exact they have to be, the bound alone decides.
A program may use at most 64 MiB of HBM per device.

```python
import math
import jax
import jax.numpy as jnp
import numpy as np
from jax import lax

CX = 64
CY = 128
ITERS = 2
SRC_DEV = 1024
SURF_TILES = 16
TILE_POINTS = 128
BOXES = 512
CAP = 64
NX = 2048
NY = 2048
SRC_TOTAL = 524288
TILE_COUNT = 8192
SURF_TOTAL = 1048576
N_GX = 32
N_GY = 16


def draw_src_count(key, part):
    base = jax.random.randint(key, (BOXES,), SRC_DEV // 4, SRC_DEV + 1)
    chosen = jax.random.randint(jax.random.fold_in(key, 7), (), 0, BOXES)
    return jnp.where(jnp.arange(BOXES) == chosen, SRC_DEV, base).astype(jnp.int32)


def node_blocks():
    block_x = jnp.arange(NX, dtype=jnp.int32) // CX
    block_y = jnp.arange(NY, dtype=jnp.int32) // CY
    return (block_x, block_y)


def draw_diag_blocks(key, part):
    first, second = jax.random.split(key)
    block_x, block_y = node_blocks()
    row_part = jax.random.uniform(jax.random.fold_in(key, 11), (NX // CX,), minval=0.0, maxval=1.0)
    col_part = jax.random.uniform(jax.random.fold_in(key, 12), (NY // CY,), minval=0.0, maxval=1.0)
    coupling_level = 0.1 + 0.4 * row_part[block_x][:, None] + 0.4 * col_part[block_y][None, :]
    coords = jnp.arange(NX, dtype=jnp.float32)[None, :, None]
    rising = 1.0 + 2.0 * coords / NX
    main = jax.random.uniform(first, (9, NX, NY), minval=6.0, maxval=10.0)
    side = coupling_level[None, :, :] + jax.random.uniform(second, (9, NX, NY), minval=-0.05, maxval=0.05)
    onmain = (jnp.arange(9) % 4 == 0)[:, None, None]
    return jnp.where(onmain, main * rising, side).astype(jnp.float32)


def draw_edge_blocks(key, part):
    block_x, block_y = node_blocks()
    sign_table = 2.0 * jax.random.randint(jax.random.fold_in(key, 21), (NX // CX, NY // CY), 0, 2).astype(jnp.float32) - 1.0
    sign_field = sign_table[block_x[:, None], block_y[None, :]]
    jitter = jax.random.uniform(key, (4, 9, NX, NY), minval=-0.05, maxval=0.05)
    result = 0.25 * sign_field[None, None, :, :] + jitter
    return result.astype(jnp.float32)


def draw_src_values(key, part):
    first, second = jax.random.split(key)
    sign_row = 2.0 * jax.random.randint(second, (1, SRC_TOTAL), 0, 2).astype(jnp.float32) - 1.0
    magnitude = jnp.minimum(8.0 * jnp.abs(jax.random.normal(first, (3, SRC_TOTAL))), 48.0)
    return (magnitude * sign_row).astype(jnp.float32)


def place_ends(drawn, rng, low, top_value):
    index_at = [jax.random.randint(jax.random.fold_in(rng, axis), (), 0, length) for axis, length in enumerate(drawn.shape)]
    main_axis = drawn.shape.index(max(drawn.shape))
    neighbour = index_at[:main_axis] + [(index_at[main_axis] + 1) % drawn.shape[main_axis]] + index_at[main_axis + 1:]
    return drawn.at[tuple(index_at)].set(low).at[tuple(neighbour)].set(top_value)


def block_scale(own_key, shape, cuts, smallest, largest):
    loudness, own = 1.0, jax.random.fold_in(own_key, 6)
    for dim, parts in cuts:
        heights = jnp.exp(jax.random.uniform(jax.random.fold_in(own, dim), (parts,), jnp.float32, smallest / len(cuts), largest / len(cuts)))
        loudness = loudness * jnp.repeat(heights, shape[dim] // parts).reshape([-1 if axis == dim else 1 for axis in range(len(shape))])
    return loudness


def deal_out(key, own, number, rows, amount, top, limit, slope):
    order = jax.random.permutation(key, amount)
    heavy_load, common = shares(amount, rows * top, limit, slope, True), shares(amount, rows * top, limit, slope, False)
    places = jnp.arange(amount)

    def named(sizes, rotation):
        used = int((sizes > 0).sum())
        fixed = max(1, used // 4)
        passed = fixed + (places - fixed + rotation * (used - fixed)) % max(1, amount - fixed)
        return jnp.zeros((amount,), jnp.int32).at[order[jnp.where(places < fixed, places, passed)]].set(jnp.asarray(sizes, jnp.int32))

    sizes = jnp.where(number % 4 == 0, named(heavy_load, number // 4), named(common, number - number // 4 - 1))
    mixed = jax.random.permutation(jax.random.fold_in(own, 3), amount)
    giver, sink = mixed[0:amount // 2 * 2:2], mixed[1:amount // 2 * 2:2]
    margin = jnp.minimum(sizes[giver] - 1, limit - sizes[sink]) // 2
    margin = jnp.where((giver == order[0]) | (sink == order[0]) | (sizes[sink] == 0), 0, jnp.maximum(margin, 0))
    passed = jax.random.randint(jax.random.fold_in(own, 4), (amount // 2,), 0, 1 << 20) % (margin + 1)
    sizes = sizes.at[giver].add(-passed).at[sink].add(passed)
    members = jnp.searchsorted(jnp.cumsum(sizes), jnp.arange(rows * top), side="right").astype(jnp.int32)
    listing = members.reshape(top, rows).T
    listing = listing[jax.random.permutation(jax.random.fold_in(own, 1), rows)]
    rotation = jax.random.randint(jax.random.fold_in(own, 2), (rows, 1), 0, top)
    return jnp.take_along_axis(listing, (jnp.arange(top)[None, :] + rotation) % top, axis=1)


def shares(number_of, total, reach, slope, full):
    loads = [(1 << 20) // math.isqrt(grade ** slope) + 1 for grade in range(1, number_of + 1)]
    largest = reach if full else min(reach, max(-(-total // number_of), total * loads[0] // sum(loads)))
    least = 1 if total - largest >= number_of - 1 else 0
    holding, spare = [largest] + [least] * (number_of - 1), total - largest - least * (number_of - 1)
    while spare > 0:
        movable = [i for i in range(1, number_of) if holding[i] < largest] or [i for i in range(1, number_of) if holding[i] < reach]
        pool, left = sum([loads[i] for i in movable]), spare
        for i in movable:
            extra = min(reach - holding[i], max(1, left * loads[i] // pool), spare)
            holding[i] = holding[i] + extra
            spare = spare - extra
    return np.array(holding)


def setup_inputs(seed: int = 0) -> dict:
    seeds = jax.random.split(jax.random.key(seed), 11)
    diag_blocks = draw_diag_blocks(jax.random.fold_in(seeds[10], 71), 0)
    edge_blocks = draw_edge_blocks(jax.random.fold_in(seeds[10], 71), 0)
    edge_mask = place_ends((jax.random.randint(seeds[2], (4, NX, NY), 0, 4) < 3).astype(jnp.int32), jax.random.fold_in(seeds[2], 1), 0, 1)
    src_values = draw_src_values(jax.random.fold_in(seeds[10], 71), 0)
    src_owner_keys = jax.random.split(jax.random.fold_in(seeds[4], 1), SRC_TOTAL // SRC_DEV)
    src_owner_turns = jax.random.permutation(jax.random.fold_in(seeds[4], 3), SRC_TOTAL // SRC_DEV)
    src_owner = jax.vmap(lambda own, number: deal_out(jax.random.fold_in(seeds[4], 2), own, number, SRC_DEV, N_GX, 1, CAP, 2))(src_owner_keys, src_owner_turns).reshape((SRC_TOTAL, 1))
    src_node = place_ends(jax.random.randint(seeds[5], (SRC_TOTAL,), 0, CX * CY), jax.random.fold_in(seeds[5], 1), 0, (CX * CY) - 1).astype(jnp.int32)
    src_count = draw_src_count(jax.random.fold_in(seeds[10], 71), 0)
    surf_node = place_ends(jax.random.randint(seeds[7], (SURF_TOTAL,), 0, CX * CY), jax.random.fold_in(seeds[7], 1), 0, (CX * CY) - 1).astype(jnp.int32)
    surf_param = jnp.clip(1.0 * jax.random.uniform(seeds[8], (3, SURF_TOTAL), jnp.float32) ** block_scale(seeds[8], (3, SURF_TOTAL), ((1, 512),), -0.2, 0.2), 0.0, 1.0)
    tile_box = place_ends(jax.random.randint(seeds[9], (TILE_COUNT,), 0, BOXES), jax.random.fold_in(seeds[9], 1), 0, BOXES - 1).astype(jnp.int32)
    return {"diag_blocks": diag_blocks, "edge_blocks": edge_blocks, "edge_mask": edge_mask, "src_values": src_values, "src_owner": src_owner, "src_node": src_node, "src_count": src_count, "surf_node": surf_node, "surf_param": surf_param, "tile_box": tile_box}


def block_product(blocks, field):
    return jnp.stack([blocks[row] * field[0] + blocks[3 + row] * field[1] + blocks[6 + row] * field[2] for row in range(3)])


def apply_transposed_operator(field, diag_blocks, masked):
    result = block_product(diag_blocks, field)
    upper_x = jnp.pad(block_product(masked[0], field), ((0, 0), (1, 0), (0, 0)))[:, :-1, :]
    lower_x = jnp.pad(block_product(masked[1], field), ((0, 0), (0, 1), (0, 0)))[:, 1:, :]
    upper_y = jnp.pad(block_product(masked[2], field), ((0, 0), (0, 0), (1, 0)))[:, :, :-1]
    lower_y = jnp.pad(block_product(masked[3], field), ((0, 0), (0, 0), (0, 1)))[:, :, 1:]
    return result + upper_x + lower_x + upper_y + lower_y


def bernstein(coord):
    other = 1.0 - coord
    return jnp.stack([other * other * other, 3.0 * coord * other * other, 3.0 * coord * coord * other, coord * coord * coord])


def tile_weights(params):
    first = bernstein(params[0])
    second = bernstein(params[1])
    third = bernstein(params[2])
    table = first[:, None, None, :] * second[None, :, None, :] * third[None, None, :, :]
    return table.reshape(64, -1)


def reference(diag_blocks, edge_blocks, edge_mask, src_values, src_owner, src_node, src_count, surf_node, surf_param, tile_box):
    masked = edge_blocks * edge_mask.astype(jnp.float32)[:, None]
    total_rows = src_node.shape[0]
    rows = jnp.arange(total_rows, dtype=jnp.int32)
    sender = rows // SRC_DEV
    live = (rows % SRC_DEV) < src_count[sender]
    column = sender % N_GY
    xs = src_owner[:, 0] * CX + src_node // CY
    ys = column * CY + src_node % CY
    load = jnp.zeros((3, NX, NY), jnp.float32).at[:, xs, ys].add(src_values * live.astype(jnp.float32))
    scale = jnp.stack([diag_blocks[0], diag_blocks[4], diag_blocks[8]])
    solution = jnp.zeros_like(load)
    residual = load
    precond = residual / scale
    search = precond
    norm_now = jnp.sum(residual * precond)
    for sweep in range(ITERS):
        image = apply_transposed_operator(search, diag_blocks, masked)
        step_size = norm_now / jnp.sum(search * image)
        solution = solution + step_size * search
        residual = residual - step_size * image
        if sweep + 1 < ITERS:
            precond = residual / scale
            norm_next = jnp.sum(residual * precond)
            search = precond + (norm_next / norm_now) * search
            norm_now = norm_next
    points = surf_node.shape[0]
    holder = jnp.arange(points, dtype=jnp.int32) // (SURF_TILES * TILE_POINTS)
    node_x = (holder // N_GY) * CX + surf_node // CY
    node_y = (holder % N_GY) * CY + surf_node % CY
    design_sensitivity = solution[:, node_x, node_y]
    tile_weight_values = tile_weights(surf_param)
    surface_tiles = tile_box.shape[0]
    series_terms = jnp.einsum('bqe,iqe->qib', tile_weight_values.reshape(64, surface_tiles, TILE_POINTS), design_sensitivity.reshape(3, surface_tiles, TILE_POINTS), precision=lax.Precision.HIGHEST).reshape(surface_tiles, 192)
    boxed = jax.ops.segment_sum(series_terms, tile_box, num_segments=BOXES)
    return solution, boxed
```

```python
import functools

import jax
import jax.numpy as jnp
from jax import lax
from jax.experimental import pallas as pl
from jax.experimental.pallas import tpu as pltpu
from jax.sharding import PartitionSpec as P

F32 = jnp.float32
BF16 = jnp.bfloat16
NT = (((1,), (1,)), ((), ()))


def halves(value):
    high = value.astype(BF16)
    low = (value - high.astype(F32)).astype(BF16)
    return high, low


def iota(shape, dim):
    return lax.broadcasted_iota(jnp.int32, shape, dim)


def mm(a, b, dims=(((1,), (0,)), ((), ()))):
    return lax.dot_general(a, b, dims, preferred_element_type=F32)


def kernel(
    sizes,
    count_ref,
    box_ref,
    diag_ref,
    edge_ref,
    mask_ref,
    val_ref,
    owner_ref,
    node_ref,
    surf_ref,
    param_ref,
    field_ref,
    grad_ref,
    v8_ref,
    bin_ref,
    ry_ref,
    pack_ref,
    rx_ref,
    halo_s,
    halo_r,
    sum_s,
    sum_y,
    sum_x,
    sum_z,
    sum_c,
    weight_ref,
    by_ref,
    bxs_ref,
    bxr_ref,
    bzs_ref,
    bzr_ref,
    bcs_ref,
    bcr_ref,
    send_sem,
    recv_sem,
):
    yn, xn, zn, cn = sizes
    gx, gy = lax.axis_index("gx"), lax.axis_index("gy")
    my, mx = gx // xn, gx % xn
    mz, mc = gy // cn, gy % cn

    def to_y(d):
        return (((my + d) % yn) * xn + mx, gy)

    def to_x(d):
        return (my * xn + (mx + d) % xn, gy)

    def to_z(d):
        return (gx, ((mz + d) % zn) * cn + mc)

    def to_c(d):
        return (gx, mz * cn + (mc + d) % cn)

    around = [
        ((gx + 1) % (yn * xn), gy),
        ((gx + yn * xn - 1) % (yn * xn), gy),
        (gx, (gy + 1) % (zn * cn)),
        (gx, (gy + zn * cn - 1) % (zn * cn)),
    ]
    axes = [(to_y, yn), (to_x, xn), (to_z, zn), (to_c, cn)]

    barrier = pltpu.get_barrier_semaphore()
    greeted = 0
    for target, size in axes:
        for d in range(1, size):
            pl.semaphore_signal(
                barrier, inc=1, device_id=target(d), device_id_type=pl.DeviceIdType.MESH
            )
            greeted += 1
    for target in around:
        pl.semaphore_signal(barrier, inc=1, device_id=target, device_id_type=pl.DeviceIdType.MESH)
        greeted += 1

    used = [0]

    def send(src, dst, target):
        slot = used[0]
        used[0] += 1
        copy = pltpu.make_async_remote_copy(
            src_ref=src,
            dst_ref=dst,
            send_sem=send_sem.at[slot],
            recv_sem=recv_sem.at[slot],
            device_id=target,
            device_id_type=pl.DeviceIdType.MESH,
        )
        copy.start()
        return copy

    def finish(copies):
        for copy in copies:
            copy.wait()

    owners = yn * xn
    v8_ref[...] = jnp.zeros_like(v8_ref)
    v8_ref[0:3, :] = val_ref[...]
    nodes = node_ref[...]
    v8_ref[3:4, :] = (nodes >> 7).astype(F32)
    v8_ref[4:5, :] = (nodes & 127).astype(F32)
    rows = nodes.shape[1]
    live = iota((1, rows), 1) < count_ref[0]
    owner = jnp.where(live, owner_ref[...], -1)
    upper = (iota((128, 128), 0) <= iota((128, 128), 1)).astype(BF16)
    before = jnp.zeros((owners, 1), F32)
    binned = jnp.zeros((owners * 8, 128), F32)
    for b in range(rows // 128):
        cut = slice(128 * b, 128 * b + 128)
        hot = (iota((owners, 128), 0) == owner[:, cut]).astype(F32)
        order = mm(hot.astype(BF16), upper) + before
        before = before + jnp.sum(hot, axis=1, keepdims=True)
        rank = jnp.sum(hot * order, axis=0, keepdims=True) - 1.0
        place = (iota((128, 128), 0).astype(F32) == rank).astype(BF16)
        part = v8_ref[:, cut]
        spread = (hot[:, None, :] * part[None, :, :]).reshape(owners * 8, 128)
        high, low = halves(spread)
        binned = binned + mm(high, place, NT) + mm(low, place, NT)
    bin_ref[...] = binned.reshape(yn, xn, 8, 128)

    pl.semaphore_wait(barrier, greeted)
    copies = [
        send(bin_ref.at[(my + d) % yn], ry_ref.at[d], to_y(d)) for d in range(1, yn)
    ]
    ry_ref[0] = bin_ref[my]

    def bern(coord, index):
        other = 1.0 - coord
        return jnp.where(
            index == 0,
            other * other * other,
            jnp.where(
                index == 1,
                3.0 * coord * other * other,
                jnp.where(index == 2, 3.0 * coord * coord * other, coord * coord * coord),
            ),
        )

    tiles = surf_ref.shape[0]
    line = iota((64, 128), 0)

    def weights(t, carry):
        cut = pl.ds(pl.multiple_of(t * 128, 128), 128)
        first = bern(param_ref[0:1, cut], line // 16)
        second = bern(param_ref[1:2, cut], (line // 4) % 4)
        third = bern(param_ref[2:3, cut], line % 4)
        weight_ref[t] = first * second * third
        return carry

    lax.fori_loop(0, tiles, weights, 0)

    finish(copies)
    for i in range(yn // 2):
        for e in range(xn):
            pack_ref[e, i] = ry_ref[2 * i, e] + pltpu.roll(ry_ref[2 * i + 1, e], 64, 1)
    copies = [
        send(pack_ref.at[(mx + d) % xn], rx_ref.at[d], to_x(d)) for d in range(1, xn)
    ]
    rx_ref[0] = pack_ref[mx]
    finish(copies)

    per = yn // 2

    def scatter(t, total):
        tile = rx_ref[t // per, t % per]
        row_hot = iota((64, 128), 0).astype(F32) == tile[3:4, :]
        col_hot = (iota((128, 128), 0).astype(F32) == tile[4:5, :]).astype(BF16)
        left = jnp.concatenate(
            [jnp.where(row_hot, tile[c : c + 1, :], 0.0) for c in range(3)], axis=0
        )
        high, low = halves(left)
        return total + mm(high, col_hot, NT) + mm(low, col_hot, NT)

    load = lax.fori_loop(0, xn * per, scatter, jnp.zeros((192, 128), F32))
    comps = range(3)
    residual = [load[64 * c : 64 * c + 64] for c in comps]

    row_id, lane_id = iota((64, 128), 0), iota((64, 128), 1)
    same = row_id == lane_id
    zero_rows = jnp.zeros((5, 128), F32)

    def operator(field, h):
        def product(d):
            keep = mask_ref[d].astype(F32)
            return [
                keep
                * (
                    edge_ref[d, c] * field[0]
                    + edge_ref[d, 3 + c] * field[1]
                    + edge_ref[d, 6 + c] * field[2]
                )
                for c in comps
            ]

        up_x, low_x, up_y, low_y = product(0), product(1), product(2), product(3)

        def column(value, lane):
            wide = jnp.broadcast_to(value[:, lane : lane + 1], (64, 128))
            return jnp.sum(jnp.where(same, wide, 0.0), axis=0, keepdims=True)

        outgoing = [
            [up_x[c][63:64, :] for c in comps],
            [low_x[c][0:1, :] for c in comps],
            [column(up_y[c], 127) for c in comps],
            [column(low_y[c], 0) for c in comps],
        ]
        copies = []
        for k in range(4):
            halo_s[h, k] = jnp.concatenate(outgoing[k] + [zero_rows], axis=0)
        for k in range(4):
            copies.append(send(halo_s.at[h, k], halo_r.at[h, k], around[k]))
        inner = [
            diag_ref[c] * field[0] + diag_ref[3 + c] * field[1] + diag_ref[6 + c] * field[2]
            for c in comps
        ]
        finish(copies)
        there = [gx > 0, gx < yn * xn - 1, gy > 0, gy < zn * cn - 1]
        got = [halo_r[h, k] * there[k].astype(F32) for k in range(4)]

        def upright(row):
            wide = jnp.broadcast_to(row, (64, 128))
            return jnp.sum(jnp.where(same, wide, 0.0), axis=1, keepdims=True)

        return [
            inner[c]
            + jnp.where(row_id == 0, got[0][c : c + 1, :], pltpu.roll(up_x[c], 1, 0))
            + jnp.where(row_id == 63, got[1][c : c + 1, :], pltpu.roll(low_x[c], 63, 0))
            + jnp.where(lane_id == 0, upright(got[2][c : c + 1, :]), pltpu.roll(up_y[c], 1, 1))
            + jnp.where(
                lane_id == 127, upright(got[3][c : c + 1, :]), pltpu.roll(low_y[c], 127, 1)
            )
            for c in comps
        ]

    def partial(pairs):
        total = None
        for a, b in pairs:
            for c in comps:
                total = a[c] * b[c] if total is None else total + a[c] * b[c]
        return jnp.sum(total, axis=0, keepdims=True)

    def total_sums(lines, h):
        pad = jnp.zeros((8 - len(lines), 128), F32)
        total = jnp.concatenate(lines + [pad], axis=0)
        for stage, landing in enumerate((sum_y, sum_x, sum_z, sum_c)):
            target, size = axes[stage]
            sum_s[h, stage] = total
            copies = [
                send(sum_s.at[h, stage], landing.at[h, d - 1], target(d)) for d in range(1, size)
            ]
            finish(copies)
            for d in range(1, size):
                total = total + landing[h, d - 1]
        total = jnp.sum(total, axis=1, keepdims=True)
        return [total[q : q + 1, :] for q in range(len(lines))]

    scale = [diag_ref[0], diag_ref[4], diag_ref[8]]
    search = [residual[c] / scale[c] for c in comps]
    image = operator(search, 0)
    norm, bend = total_sums([partial([(residual, search)]), partial([(search, image)])], 0)
    step = norm / bend
    residual = [residual[c] - step * image[c] for c in comps]
    precond = [residual[c] / scale[c] for c in comps]
    image_z = operator(precond, 1)
    norm_next, bend_z, bend_mix = total_sums(
        [
            partial([(residual, precond)]),
            partial([(precond, image_z)]),
            partial([(precond, image), (search, image_z)]),
        ],
        1,
    )
    turn = norm_next / norm
    step_next = norm_next / (bend_z + turn * bend_mix + turn * turn * bend)
    answer = [
        step * search[c] + step_next * (precond[c] + turn * search[c]) for c in comps
    ]
    for c in comps:
        field_ref[c] = answer[c]

    high, low = halves(jnp.concatenate(answer, axis=0))
    stacked = jnp.concatenate([high, low], axis=0)

    def term(t, total):
        node = surf_ref[pl.ds(t, 1), :]
        row_hot = iota((64, 128), 0) == (node >> 7)
        col_hot = (iota((128, 128), 0) == (node & 127)).astype(BF16)
        picked = mm(stacked, col_hot)
        weight = weight_ref[t]
        parts = []
        for c in comps:
            at = picked[64 * c : 64 * c + 64] + picked[192 + 64 * c : 256 + 64 * c]
            value = jnp.sum(jnp.where(row_hot, at, 0.0), axis=0, keepdims=True)
            parts.append(weight * value)
        parts.append(jnp.where(lane_id == 0, box_ref[t].astype(F32), 0.0))
        part_high, part_low = halves(jnp.concatenate(parts, axis=0))
        here = (iota((tiles, 128), 0) == t).astype(BF16)
        return total + mm(here, part_high, NT) + mm(here, part_low, NT)

    terms = lax.fori_loop(0, tiles, term, jnp.zeros((tiles, 256), F32))
    by_ref[0] = terms
    copies = [send(by_ref.at[0], by_ref.at[d], to_y(d)) for d in range(1, yn)]
    finish(copies)
    every = by_ref[...].reshape(yn * tiles, 256)
    per_y, per_x, per_z = xn * zn * cn, zn * cn, cn
    box = every[:, 192:193]
    wanted = (my * per_y + iota((yn * tiles, 128), 1)).astype(F32)
    chosen = jnp.transpose((box == wanted).astype(F32))[:per_y].astype(BF16)
    high, low = halves(every)
    dense = mm(chosen, high) + mm(chosen, low)
    bxs_ref[...] = dense.reshape(xn, per_x, 256)
    copies = [send(bxs_ref.at[(mx + d) % xn], bxr_ref.at[d - 1], to_x(d)) for d in range(1, xn)]
    dense = bxs_ref[mx]
    finish(copies)
    for d in range(1, xn):
        dense = dense + bxr_ref[d - 1]
    bzs_ref[...] = jnp.zeros_like(bzs_ref)
    for k in range(zn):
        bzs_ref[k, 0:per_z, :] = dense[k * per_z : (k + 1) * per_z, :]
    copies = [send(bzs_ref.at[(mz + d) % zn], bzr_ref.at[d - 1], to_z(d)) for d in range(1, zn)]
    dense = bzs_ref[mz]
    finish(copies)
    for d in range(1, zn):
        dense = dense + bzr_ref[d - 1]
    bcs_ref[...] = dense
    copies = [send(bcs_ref, bcr_ref, to_c(1))]
    finish(copies)
    dense = dense + bcr_ref[...]
    grad_ref[...] = jnp.where(mc == 0, dense[0:1, 0:192], dense[1:2, 0:192])


def per_device(
    sizes,
    diag_blocks,
    edge_blocks,
    edge_mask,
    src_values,
    src_owner,
    src_node,
    src_count,
    surf_node,
    surf_param,
    tile_box,
):
    yn, xn, zn, cn = sizes
    tiles = tile_box.shape[0]
    rows = src_node.shape[0]
    vmem = pl.BlockSpec(memory_space=pltpu.VMEM)
    smem = pl.BlockSpec(memory_space=pltpu.SMEM)
    copies = 2 * (yn + xn - 2 + 2) + (yn + xn + zn + cn - 4) * 3 + 8
    per_x = zn * cn

    def buf(*shape):
        return pltpu.VMEM(shape, F32)

    return pl.pallas_call(
        functools.partial(kernel, sizes),
        out_shape=(
            jax.ShapeDtypeStruct(diag_blocks.shape[:0] + (3,) + diag_blocks.shape[1:], F32),
            jax.ShapeDtypeStruct((1, 192), F32),
        ),
        in_specs=[smem, smem] + [vmem] * 8,
        out_specs=(vmem, vmem),
        scratch_shapes=[
            buf(8, rows),
            buf(yn, xn, 8, 128),
            buf(yn, xn, 8, 128),
            buf(xn, yn // 2, 8, 128),
            buf(xn, yn // 2, 8, 128),
            buf(2, 4, 8, 128),
            buf(2, 4, 8, 128),
            buf(2, 4, 8, 128),
            buf(2, yn - 1, 8, 128),
            buf(2, xn - 1, 8, 128),
            buf(2, zn - 1, 8, 128),
            buf(2, cn - 1, 8, 128),
            buf(tiles, 64, 128),
            buf(yn, tiles, 256),
            buf(xn, per_x, 256),
            buf(xn - 1, per_x, 256),
            buf(zn, 8, 256),
            buf(zn - 1, 8, 256),
            buf(8, 256),
            buf(8, 256),
            pltpu.SemaphoreType.DMA((copies,)),
            pltpu.SemaphoreType.DMA((copies,)),
        ],
        compiler_params=pltpu.CompilerParams(
            collective_id=0, has_side_effects=True, vmem_limit_bytes=32 * 2**20
        ),
    )(
        src_count,
        tile_box,
        diag_blocks,
        edge_blocks,
        edge_mask,
        src_values,
        src_owner.reshape(1, rows),
        src_node.reshape(1, rows),
        surf_node.reshape(tiles, 128),
        surf_param,
    )


def solution(mesh):
    across, along = mesh.shape["gx"], mesh.shape["gy"]
    xn = 4 if across >= 16 else 2
    sizes = (across // xn, xn, along // 2, 2)
    return jax.shard_map(
        functools.partial(per_device, sizes),
        mesh=mesh,
        in_specs=(
            P(None, "gx", "gy"),
            P(None, None, "gx", "gy"),
            P(None, "gx", "gy"),
            P(None, ("gx", "gy")),
            P(("gx", "gy"), None),
            P(("gx", "gy")),
            P(("gx", "gy")),
            P(("gx", "gy")),
            P(None, ("gx", "gy")),
            P(("gx", "gy")),
        ),
        out_specs=(P(None, "gx", "gy"), P(("gx", "gy"), None)),
        check_vma=False,
    )
```

```python
import functools

import jax
import jax.numpy as jnp
from jax import lax
from jax.experimental import pallas as pl
from jax.experimental.pallas import tpu as pltpu
from jax.sharding import PartitionSpec as P

F32 = jnp.float32
BF16 = jnp.bfloat16
NT = (((1,), (1,)), ((), ()))


def halves(value):
    high = value.astype(BF16)
    low = (value - high.astype(F32)).astype(BF16)
    return high, low


def iota(shape, dim):
    return lax.broadcasted_iota(jnp.int32, shape, dim)


def mm(a, b, dims=(((1,), (0,)), ((), ()))):
    return lax.dot_general(a, b, dims, preferred_element_type=F32)


def kernel(
    sizes,
    count_hbm,
    box_hbm,
    diag_hbm,
    edge_hbm,
    mask_hbm,
    val_hbm,
    owner_hbm,
    node_hbm,
    surf_hbm,
    param_hbm,
    field_ref,
    grad_ref,
    count_ref,
    box_ref,
    diag_ref,
    edge_ref,
    mask_ref,
    val_ref,
    owner_ref,
    node_ref,
    surf_ref,
    param_ref,
    v8_ref,
    bin_ref,
    ry_ref,
    rx_ref,
    halo_s,
    halo_r,
    sum_s,
    sum_y,
    sum_x,
    sum_z,
    sum_c,
    weight_ref,
    by_ref,
    bxs_ref,
    bxr_ref,
    bzs_ref,
    bzr_ref,
    bcs_ref,
    bcr_ref,
    load_sem,
    send_sem,
    recv_sem,
):
    yn, xn, zn, cn = sizes
    gx, gy = lax.axis_index("gx"), lax.axis_index("gy")
    my, mx = gx // xn, gx % xn
    mz, mc = gy // cn, gy % cn

    def to_y(d):
        return (((my + d) % yn) * xn + mx, gy)

    def to_x(d):
        return (my * xn + (mx + d) % xn, gy)

    def to_z(d):
        return (gx, ((mz + d) % zn) * cn + mc)

    def to_c(d):
        return (gx, mz * cn + (mc + d) % cn)

    around = [
        ((gx + 1) % (yn * xn), gy),
        ((gx + yn * xn - 1) % (yn * xn), gy),
        (gx, (gy + 1) % (zn * cn)),
        (gx, (gy + zn * cn - 1) % (zn * cn)),
    ]
    axes = [(to_y, yn), (to_x, xn), (to_z, zn), (to_c, cn)]

    moved = [
        (count_hbm, count_ref),
        (owner_hbm, owner_ref),
        (node_hbm, node_ref),
        (val_hbm, val_ref),
        (param_hbm, param_ref),
        (mask_hbm, mask_ref),
        (edge_hbm, edge_ref),
        (diag_hbm, diag_ref),
        (surf_hbm, surf_ref),
        (box_hbm, box_ref),
    ]
    loads = [
        pltpu.make_async_copy(src, dst, load_sem.at[n]) for n, (src, dst) in enumerate(moved)
    ]
    for copy in loads:
        copy.start()

    barrier = pltpu.get_barrier_semaphore()
    greeted = 0
    for target, size in axes:
        for d in range(1, size):
            pl.semaphore_signal(
                barrier, inc=1, device_id=target(d), device_id_type=pl.DeviceIdType.MESH
            )
            greeted += 1
    for target in around:
        pl.semaphore_signal(barrier, inc=1, device_id=target, device_id_type=pl.DeviceIdType.MESH)
        greeted += 1

    used = [0]

    def send(src, dst, target):
        slot = used[0]
        used[0] += 1
        copy = pltpu.make_async_remote_copy(
            src_ref=src,
            dst_ref=dst,
            send_sem=send_sem.at[slot],
            recv_sem=recv_sem.at[slot],
            device_id=target,
            device_id_type=pl.DeviceIdType.MESH,
        )
        copy.start()
        return copy

    def finish(copies):
        for copy in copies:
            copy.wait()

    owners = yn * xn
    for copy in loads[:4]:
        copy.wait()
    v8_ref[...] = jnp.zeros_like(v8_ref)
    nodes = node_ref[...]
    v8_ref[0, 0:1, :] = val_ref[0:1, :]
    v8_ref[0, 1:2, :] = val_ref[2:3, :]
    v8_ref[1, 0:1, :] = val_ref[1:2, :]
    v8_ref[1, 1:2, :] = nodes.astype(F32)
    rows = nodes.shape[1]
    live = iota((1, rows), 1) < count_ref[...]
    owner = jnp.where(live, owner_ref[...], -1)
    upper = (iota((128, 128), 0) <= iota((128, 128), 1)).astype(BF16)
    before = jnp.zeros((owners, 1), F32)
    binned = jnp.zeros((owners * 8, 128), F32)
    for b in range(rows // 128):
        cut = slice(128 * b, 128 * b + 128)
        hot = (iota((owners, 128), 0) == owner[:, cut]).astype(F32)
        order = mm(hot.astype(BF16), upper) + before
        before = before + jnp.sum(hot, axis=1, keepdims=True)
        rank = jnp.sum(hot * order, axis=0, keepdims=True) - 1.0
        for half in range(2):
            spot = jnp.where(rank < 0.0, -1.0, rank + 64.0 * half)
            place = (iota((128, 128), 0).astype(F32) == spot).astype(BF16)
            part = v8_ref[half, :, cut]
            spread = (hot[:, None, :] * part[None, :, :]).reshape(owners * 8, 128)
            high, low = halves(spread)
            binned = binned + mm(high, place, NT) + mm(low, place, NT)
    bin_ref[...] = binned.reshape(yn, xn, 8, 128)[:, :, 0:2, :]

    pl.semaphore_wait(barrier, greeted)
    copies = [
        send(bin_ref.at[(my + d) % yn], ry_ref.at[d], to_y(d)) for d in range(1, yn)
    ]
    ry_ref[0] = bin_ref[my]

    def bern(coord, index):
        other = 1.0 - coord
        return jnp.where(
            index == 0,
            other * other * other,
            jnp.where(
                index == 1,
                3.0 * coord * other * other,
                jnp.where(index == 2, 3.0 * coord * coord * other, coord * coord * coord),
            ),
        )

    tiles = surf_ref.shape[0]
    line = iota((64, 128), 0)

    def weights(t, carry):
        cut = pl.ds(pl.multiple_of(t * 128, 128), 128)
        first = bern(param_ref[0:1, cut], line // 16)
        second = bern(param_ref[1:2, cut], (line // 4) % 4)
        third = bern(param_ref[2:3, cut], line % 4)
        weight_ref[t] = first * second * third
        return carry

    loads[4].wait()
    lax.fori_loop(0, tiles, weights, 0)

    for copy in loads[5:]:
        copy.wait()
    for d in range(4):
        keep = mask_ref[d].astype(F32)
        for n in range(9):
            edge_ref[d, n] = edge_ref[d, n] * keep

    finish(copies)
    copies = [
        send(ry_ref.at[:, (mx + d) % xn], rx_ref.at[d], to_x(d)) for d in range(1, xn)
    ]
    rx_ref[0] = ry_ref[:, mx]
    finish(copies)

    per = yn // 2
    left_half = iota((2, 128), 1) < 64

    def scatter(t, total):
        one, two = rx_ref[t // per, 2 * (t % per)], rx_ref[t // per, 2 * (t % per) + 1]
        near = jnp.where(left_half, one, pltpu.roll(two, 64, 1))
        far = jnp.where(left_half, pltpu.roll(one, 64, 1), two)
        node = far[1:2, :].astype(jnp.int32)
        row_hot = iota((64, 128), 0) == (node >> 7)
        col_hot = (iota((128, 128), 0) == (node & 127)).astype(BF16)
        values = [near[0:1, :], far[0:1, :], near[1:2, :]]
        left = jnp.concatenate([jnp.where(row_hot, v, 0.0) for v in values], axis=0)
        high, low = halves(left)
        return total + mm(high, col_hot, NT) + mm(low, col_hot, NT)

    load = lax.fori_loop(0, xn * per, scatter, jnp.zeros((192, 128), F32))
    comps = range(3)
    residual = [load[64 * c : 64 * c + 64] for c in comps]

    row_id, lane_id = iota((64, 128), 0), iota((64, 128), 1)
    same = row_id == lane_id
    zero_rows = jnp.zeros((5, 128), F32)

    def operator(field, h):
        def product(d):
            return [
                edge_ref[d, c] * field[0]
                + edge_ref[d, 3 + c] * field[1]
                + edge_ref[d, 6 + c] * field[2]
                for c in comps
            ]

        up_x, low_x, up_y, low_y = product(0), product(1), product(2), product(3)

        def column(value, lane):
            wide = jnp.broadcast_to(value[:, lane : lane + 1], (64, 128))
            return jnp.sum(jnp.where(same, wide, 0.0), axis=0, keepdims=True)

        outgoing = [
            [up_x[c][63:64, :] for c in comps],
            [low_x[c][0:1, :] for c in comps],
            [column(up_y[c], 127) for c in comps],
            [column(low_y[c], 0) for c in comps],
        ]
        copies = []
        for k in range(4):
            halo_s[h, k] = jnp.concatenate(outgoing[k] + [zero_rows], axis=0)
        for k in range(4):
            copies.append(send(halo_s.at[h, k], halo_r.at[h, k], around[k]))
        inner = [
            sum(diag_ref[3 * k + c] * field[k] for k in comps if k != c) for c in comps
        ]
        finish(copies)
        there = [gx > 0, gx < yn * xn - 1, gy > 0, gy < zn * cn - 1]
        got = [halo_r[h, k] * there[k].astype(F32) for k in range(4)]

        def upright(row):
            wide = jnp.broadcast_to(row, (64, 128))
            return jnp.sum(jnp.where(same, wide, 0.0), axis=1, keepdims=True)

        return [
            inner[c]
            + jnp.where(row_id == 0, got[0][c : c + 1, :], pltpu.roll(up_x[c], 1, 0))
            + jnp.where(row_id == 63, got[1][c : c + 1, :], pltpu.roll(low_x[c], 63, 0))
            + jnp.where(lane_id == 0, upright(got[2][c : c + 1, :]), pltpu.roll(up_y[c], 1, 1))
            + jnp.where(
                lane_id == 127, upright(got[3][c : c + 1, :]), pltpu.roll(low_y[c], 127, 1)
            )
            for c in comps
        ]

    def partial(a, b):
        return jnp.sum(a[0] * b[0] + a[1] * b[1] + a[2] * b[2], axis=0, keepdims=True)

    scale = [diag_ref[0], diag_ref[4], diag_ref[8]]
    search = [residual[c] / scale[c] for c in comps]
    other = operator(search, 0)
    second = [other[c] / scale[c] for c in comps]
    third = operator(second, 1)
    lines = [
        partial(search, residual),
        partial(search, other),
        partial(second, other),
        partial(search, third),
        partial(second, third),
    ]
    total = jnp.concatenate(lines + [jnp.zeros((8 - len(lines), 128), F32)], axis=0)
    for shift in (64, 32, 16):
        total = total + pltpu.roll(total, shift, 1)
    group = iota((8, 128), 1) // 16 == iota((8, 128), 0)
    total = jnp.sum(jnp.where(group, total, 0.0), axis=0, keepdims=True)

    pieces = halves(jnp.concatenate(search, axis=0)) + halves(jnp.concatenate(second, axis=0))
    stacked = jnp.concatenate(pieces, axis=0)

    def term(t, terms):
        node = surf_ref[pl.ds(t, 1), :]
        row_hot = iota((64, 128), 0) == (node >> 7)
        col_hot = (iota((128, 128), 0) == (node & 127)).astype(BF16)
        picked = mm(stacked, col_hot)
        weight = weight_ref[t]
        parts = []
        for first in (0, 384):
            for c in comps:
                at = first + 64 * c
                both = picked[at : at + 64] + picked[at + 192 : at + 256]
                value = jnp.sum(jnp.where(row_hot, both, 0.0), axis=0, keepdims=True)
                parts.append(weight * value)
        high, low = halves(jnp.concatenate(parts, axis=0))
        here = (iota((tiles, 128), 0) == t).astype(BF16)
        return terms + mm(here, high, NT) + mm(here, low, NT)

    terms = jnp.zeros((tiles, 384), F32)
    share = tiles // 4
    for stage, landing in enumerate((sum_y, sum_x, sum_z, sum_c)):
        target, size = axes[stage]
        sum_s[stage] = total
        copies = [send(sum_s.at[stage], landing.at[d - 1], target(d)) for d in range(1, size)]
        terms = lax.fori_loop(stage * share, (stage + 1) * share, term, terms)
        finish(copies)
        for d in range(1, size):
            total = total + landing[d - 1]
    total = jnp.where(group, jnp.broadcast_to(total, (8, 128)), 0.0)
    total = jnp.sum(total, axis=1, keepdims=True)
    norm, bend_a, bend_b, bend_c, bend_d = [total[q : q + 1, :] for q in range(5)]

    whole = norm + bend_a
    step = norm / whole
    rest = bend_a / whole
    norm_next = (norm / whole) * ((norm * bend_b - bend_a * bend_a) / whole)
    turn = norm_next / norm
    front = rest + turn
    bend_next = (
        front * front * whole
        - front * step * (2.0 * bend_a + bend_c + bend_b)
        + step * step * (bend_b + bend_d)
    )
    step_next = norm_next / bend_next
    alpha = step + step_next * front
    gamma = step * step_next

    match = iota((tiles, tiles), 0) == iota((tiles, tiles), 1)
    wide = jnp.broadcast_to(box_ref[...].astype(F32), (tiles, tiles))
    boxes = jnp.sum(jnp.where(match, wide, 0.0), axis=1, keepdims=True)
    terms = alpha * terms[:, 0:192] - gamma * terms[:, 192:384]
    terms = jnp.concatenate([terms, jnp.broadcast_to(boxes, (tiles, 64))], axis=1)
    by_ref[0] = terms
    copies = [send(by_ref.at[0], by_ref.at[d], to_y(d)) for d in range(1, yn)]
    for c in comps:
        field_ref[c] = alpha * search[c] - gamma * second[c]
    finish(copies)
    every = by_ref[...].reshape(yn * tiles, 256)
    per_y, per_x, per_z = xn * zn * cn, zn * cn, cn
    box = every[:, 192:193]
    wanted = (my * per_y + iota((yn * tiles, 128), 1)).astype(F32)
    chosen = jnp.transpose((box == wanted).astype(F32))[:per_y].astype(BF16)
    high, low = halves(every)
    dense = mm(chosen, high) + mm(chosen, low)
    bxs_ref[...] = dense.reshape(xn, per_x, 256)
    copies = [send(bxs_ref.at[(mx + d) % xn], bxr_ref.at[d - 1], to_x(d)) for d in range(1, xn)]
    dense = bxs_ref[mx]
    finish(copies)
    for d in range(1, xn):
        dense = dense + bxr_ref[d - 1]
    for k in range(zn):
        bzs_ref[k] = dense[k * per_z : (k + 1) * per_z, :]
    copies = [send(bzs_ref.at[(mz + d) % zn], bzr_ref.at[d - 1], to_z(d)) for d in range(1, zn)]
    dense = bzs_ref[mz]
    finish(copies)
    for d in range(1, zn):
        dense = dense + bzr_ref[d - 1]
    bcs_ref[...] = jnp.where(mc == 0, dense[1:2, :], dense[0:1, :])
    copies = [send(bcs_ref, bcr_ref, to_c(1))]
    dense = jnp.where(mc == 0, dense[0:1, :], dense[1:2, :])
    finish(copies)
    grad_ref[...] = (dense + bcr_ref[...])[:, 0:192]


def per_device(
    sizes,
    diag_blocks,
    edge_blocks,
    edge_mask,
    src_values,
    src_owner,
    src_node,
    src_count,
    surf_node,
    surf_param,
    tile_box,
):
    yn, xn, zn, cn = sizes
    tiles = tile_box.shape[0]
    rows = src_node.shape[0]
    vmem = pl.BlockSpec(memory_space=pltpu.VMEM)
    copies = 2 * (yn + xn - 2) + (yn + xn + zn + cn - 4) * 2 + 8
    per_x = zn * cn

    def buf(*shape):
        return pltpu.VMEM(shape, F32)

    operands = (
        src_count.reshape(1, 1),
        tile_box.reshape(1, tiles),
        diag_blocks,
        edge_blocks,
        edge_mask,
        src_values,
        src_owner.reshape(1, rows),
        src_node.reshape(1, rows),
        surf_node.reshape(tiles, 128),
        surf_param,
    )
    return pl.pallas_call(
        functools.partial(kernel, sizes),
        out_shape=(
            jax.ShapeDtypeStruct((3,) + diag_blocks.shape[1:], F32),
            jax.ShapeDtypeStruct((1, 192), F32),
        ),
        in_specs=[pl.BlockSpec(memory_space=pl.ANY)] * len(operands),
        out_specs=(vmem, vmem),
        scratch_shapes=[pltpu.VMEM(x.shape, x.dtype) for x in operands]
        + [
            buf(2, 8, rows),
            buf(yn, xn, 2, 128),
            buf(yn, xn, 2, 128),
            buf(xn, yn, 2, 128),
            buf(2, 4, 8, 128),
            buf(2, 4, 8, 128),
            buf(4, 1, 128),
            buf(yn - 1, 1, 128),
            buf(xn - 1, 1, 128),
            buf(zn - 1, 1, 128),
            buf(cn - 1, 1, 128),
            buf(tiles, 64, 128),
            buf(yn, tiles, 256),
            buf(xn, per_x, 256),
            buf(xn - 1, per_x, 256),
            buf(zn, cn, 256),
            buf(zn - 1, cn, 256),
            buf(1, 256),
            buf(1, 256),
            pltpu.SemaphoreType.DMA((len(operands),)),
            pltpu.SemaphoreType.DMA((copies,)),
            pltpu.SemaphoreType.DMA((copies,)),
        ],
        compiler_params=pltpu.CompilerParams(
            collective_id=0, has_side_effects=True, vmem_limit_bytes=60 * 2**20
        ),
    )(*operands)


def solution(mesh):
    across, along = mesh.shape["gx"], mesh.shape["gy"]
    xn = 4 if across >= 16 else 2
    sizes = (across // xn, xn, along // 2, 2)
    return jax.shard_map(
        functools.partial(per_device, sizes),
        mesh=mesh,
        in_specs=(
            P(None, "gx", "gy"),
            P(None, None, "gx", "gy"),
            P(None, "gx", "gy"),
            P(None, ("gx", "gy")),
            P(("gx", "gy"), None),
            P(("gx", "gy")),
            P(("gx", "gy")),
            P(("gx", "gy")),
            P(None, ("gx", "gy")),
            P(("gx", "gy")),
        ),
        out_specs=(P(None, "gx", "gy"), P(("gx", "gy"), None)),
        check_vma=False,
    )
```

```python
import functools

import jax
import jax.numpy as jnp
from jax import lax
from jax.experimental import pallas as pl
from jax.experimental.pallas import tpu as pltpu
from jax.sharding import PartitionSpec as P

F32 = jnp.float32
BF16 = jnp.bfloat16
NT = (((1,), (1,)), ((), ()))


def halves(value):
    high = value.astype(BF16)
    low = (value - high.astype(F32)).astype(BF16)
    return high, low


def iota(shape, dim):
    return lax.broadcasted_iota(jnp.int32, shape, dim)


def mm(a, b, dims=(((1,), (0,)), ((), ()))):
    return lax.dot_general(a, b, dims, preferred_element_type=F32)


def kernel(
    sizes,
    count_hbm,
    box_hbm,
    diag_hbm,
    edge_hbm,
    mask_hbm,
    val_hbm,
    owner_hbm,
    node_hbm,
    surf_hbm,
    param_hbm,
    field_ref,
    grad_ref,
    count_ref,
    box_ref,
    diag_ref,
    edge_ref,
    mask_ref,
    val_ref,
    owner_ref,
    node_ref,
    surf_ref,
    param_ref,
    v8_ref,
    bin_ref,
    rx_ref,
    halo_s,
    halo_r,
    sum_s,
    sum_x,
    sum_y,
    weight_ref,
    by_ref,
    bxs_ref,
    bxr_ref,
    bzs_ref,
    bzr_ref,
    load_sem,
    send_sem,
    recv_sem,
):
    yn, xn, zn, cn = sizes
    gx, gy = lax.axis_index("gx"), lax.axis_index("gy")
    my, mx = gx // xn, gx % xn

    def to_y(d):
        return (((my + d) % yn) * xn + mx, gy)

    def to_x(d):
        return (my * xn + (mx + d) % xn, gy)

    across, along = yn * xn, zn * cn

    def to_gx(d):
        return ((gx + d) % across, gy)

    def to_gy(d):
        return (gx, (gy + d) % along)

    around = [
        ((gx + 1) % (yn * xn), gy),
        ((gx + yn * xn - 1) % (yn * xn), gy),
        (gx, (gy + 1) % (zn * cn)),
        (gx, (gy + zn * cn - 1) % (zn * cn)),
    ]
    axes = [(to_gx, across), (to_gy, along)]

    moved = [
        (count_hbm, count_ref),
        (owner_hbm, owner_ref),
        (node_hbm, node_ref),
        (val_hbm, val_ref),
        (param_hbm, param_ref),
        (mask_hbm, mask_ref),
        (edge_hbm, edge_ref),
        (diag_hbm, diag_ref),
        (surf_hbm, surf_ref),
        (box_hbm, box_ref),
    ]
    loads = [
        pltpu.make_async_copy(src, dst, load_sem.at[n]) for n, (src, dst) in enumerate(moved)
    ]
    for copy in loads:
        copy.start()

    barrier = pltpu.get_barrier_semaphore()
    greeted = 0
    for target, size in axes:
        for d in range(1, size):
            pl.semaphore_signal(
                barrier, inc=1, device_id=target(d), device_id_type=pl.DeviceIdType.MESH
            )
            greeted += 1

    used = [0]

    def send(src, dst, target):
        slot = used[0]
        used[0] += 1
        copy = pltpu.make_async_remote_copy(
            src_ref=src,
            dst_ref=dst,
            send_sem=send_sem.at[slot],
            recv_sem=recv_sem.at[slot],
            device_id=target,
            device_id_type=pl.DeviceIdType.MESH,
        )
        copy.start()
        return copy

    def finish(copies):
        for copy in copies:
            copy.wait()

    owners = across
    for copy in loads[:4]:
        copy.wait()
    v8_ref[...] = jnp.zeros_like(v8_ref)
    nodes = node_ref[...]
    v8_ref[0, 0:1, :] = val_ref[0:1, :]
    v8_ref[0, 1:2, :] = val_ref[2:3, :]
    v8_ref[1, 0:1, :] = val_ref[1:2, :]
    v8_ref[1, 1:2, :] = nodes.astype(F32)
    rows = nodes.shape[1]
    live = iota((1, rows), 1) < count_ref[...]
    owner = jnp.where(live, owner_ref[...], -1)
    upper = (iota((128, 128), 0) <= iota((128, 128), 1)).astype(BF16)
    before = jnp.zeros((owners, 1), F32)
    binned = jnp.zeros((owners * 8, 128), F32)
    for b in range(rows // 128):
        cut = slice(128 * b, 128 * b + 128)
        hot = (iota((owners, 128), 0) == owner[:, cut]).astype(F32)
        order = mm(hot.astype(BF16), upper) + before
        before = before + jnp.sum(hot, axis=1, keepdims=True)
        rank = jnp.sum(hot * order, axis=0, keepdims=True) - 1.0
        for half in range(2):
            spot = jnp.where(rank < 0.0, -1.0, rank + 64.0 * half)
            place = (iota((128, 128), 0).astype(F32) == spot).astype(BF16)
            part = v8_ref[half, :, cut]
            spread = (hot[:, None, :] * part[None, :, :]).reshape(owners * 8, 128)
            high, low = halves(spread)
            binned = binned + mm(high, place, NT) + mm(low, place, NT)
    bin_ref[...] = binned.reshape(owners, 8, 128)[:, 0:2, :]

    pl.semaphore_wait(barrier, greeted)
    copies = [
        send(bin_ref.at[(gx + d) % across], rx_ref.at[d], to_gx(d)) for d in range(1, across)
    ]
    rx_ref[0] = bin_ref[gx]

    def bern(coord, index):
        other = 1.0 - coord
        return jnp.where(
            index == 0,
            other * other * other,
            jnp.where(
                index == 1,
                3.0 * coord * other * other,
                jnp.where(index == 2, 3.0 * coord * coord * other, coord * coord * coord),
            ),
        )

    tiles = surf_ref.shape[0]
    line = iota((64, 128), 0)

    def weights(t, carry):
        cut = pl.ds(pl.multiple_of(t * 128, 128), 128)
        first = bern(param_ref[0:1, cut], line // 16)
        second = bern(param_ref[1:2, cut], (line // 4) % 4)
        third = bern(param_ref[2:3, cut], line % 4)
        weight_ref[t] = first * second * third
        return carry

    loads[4].wait()
    lax.fori_loop(0, tiles, weights, 0)

    for copy in loads[5:]:
        copy.wait()
    for d in range(4):
        keep = mask_ref[d].astype(F32)
        for n in range(9):
            edge_ref[d, n] = edge_ref[d, n] * keep

    finish(copies)
    left_half = iota((2, 128), 1) < 64

    def scatter(t, total):
        one, two = rx_ref[2 * t], rx_ref[2 * t + 1]
        near = jnp.where(left_half, one, pltpu.roll(two, 64, 1))
        far = jnp.where(left_half, pltpu.roll(one, 64, 1), two)
        node = far[1:2, :].astype(jnp.int32)
        row_hot = iota((64, 128), 0) == (node >> 7)
        col_hot = (iota((128, 128), 0) == (node & 127)).astype(BF16)
        values = [near[0:1, :], far[0:1, :], near[1:2, :]]
        left = jnp.concatenate([jnp.where(row_hot, v, 0.0) for v in values], axis=0)
        high, low = halves(left)
        return total + mm(high, col_hot, NT) + mm(low, col_hot, NT)

    load = lax.fori_loop(0, owners // 2, scatter, jnp.zeros((192, 128), F32))
    comps = range(3)
    residual = [load[64 * c : 64 * c + 64] for c in comps]

    row_id, lane_id = iota((64, 128), 0), iota((64, 128), 1)
    same = row_id == lane_id
    zero_rows = jnp.zeros((5, 128), F32)

    def operator(field, h):
        def product(d, part=slice(0, 64)):
            return [
                edge_ref[d, c, part] * field[0][part]
                + edge_ref[d, 3 + c, part] * field[1][part]
                + edge_ref[d, 6 + c, part] * field[2][part]
                for c in comps
            ]

        def column(value, lane):
            wide = jnp.broadcast_to(value[:, lane : lane + 1], (64, 128))
            return jnp.sum(jnp.where(same, wide, 0.0), axis=0, keepdims=True)

        def give(k, lines):
            halo_s[h, k] = jnp.concatenate(lines + [zero_rows], axis=0)
            return send(halo_s.at[h, k], halo_r.at[h, k], around[k])

        copies = [
            give(0, [line[7:8, :] for line in product(0, slice(56, 64))]),
            give(1, [line[0:1, :] for line in product(1, slice(0, 8))]),
        ]
        up_y, low_y = product(2), product(3)
        copies.append(give(2, [column(up_y[c], 127) for c in comps]))
        copies.append(give(3, [column(low_y[c], 0) for c in comps]))
        up_x, low_x = product(0), product(1)
        inner = [
            sum(diag_ref[3 * k + c] * field[k] for k in comps if k != c)
            + jnp.where(row_id == 0, 0.0, pltpu.roll(up_x[c], 1, 0))
            + jnp.where(row_id == 63, 0.0, pltpu.roll(low_x[c], 63, 0))
            + jnp.where(lane_id == 0, 0.0, pltpu.roll(up_y[c], 1, 1))
            + jnp.where(lane_id == 127, 0.0, pltpu.roll(low_y[c], 127, 1))
            for c in comps
        ]
        finish(copies)
        there = [gx > 0, gx < yn * xn - 1, gy > 0, gy < zn * cn - 1]
        got = [halo_r[h, k] * there[k].astype(F32) for k in range(4)]

        def upright(row):
            wide = jnp.broadcast_to(row, (64, 128))
            return jnp.sum(jnp.where(same, wide, 0.0), axis=1, keepdims=True)

        return [
            inner[c]
            + jnp.where(row_id == 0, got[0][c : c + 1, :], 0.0)
            + jnp.where(row_id == 63, got[1][c : c + 1, :], 0.0)
            + jnp.where(lane_id == 0, upright(got[2][c : c + 1, :]), 0.0)
            + jnp.where(lane_id == 127, upright(got[3][c : c + 1, :]), 0.0)
            for c in comps
        ]

    def partial(a, b):
        return jnp.sum(a[0] * b[0] + a[1] * b[1] + a[2] * b[2], axis=0, keepdims=True)

    scale = [diag_ref[0], diag_ref[4], diag_ref[8]]
    search = [residual[c] / scale[c] for c in comps]
    other = operator(search, 0)
    second = [other[c] / scale[c] for c in comps]
    third = operator(second, 1)
    lines = [
        partial(search, residual),
        partial(search, other),
        partial(second, other),
        partial(search, third),
        partial(second, third),
    ]
    total = jnp.concatenate(lines + [jnp.zeros((8 - len(lines), 128), F32)], axis=0)
    for shift in (64, 32, 16):
        total = total + pltpu.roll(total, shift, 1)
    group = iota((8, 128), 1) // 16 == iota((8, 128), 0)
    total = jnp.sum(jnp.where(group, total, 0.0), axis=0, keepdims=True)

    pieces = halves(jnp.concatenate(search, axis=0)) + halves(jnp.concatenate(second, axis=0))
    stacked = jnp.concatenate(pieces, axis=0)

    def term(t, terms):
        node = surf_ref[pl.ds(t, 1), :]
        row_hot = iota((64, 128), 0) == (node >> 7)
        col_hot = (iota((128, 128), 0) == (node & 127)).astype(BF16)
        picked = mm(stacked, col_hot)
        weight = weight_ref[t]
        parts = []
        for first in (0, 384):
            for c in comps:
                at = first + 64 * c
                both = picked[at : at + 64] + picked[at + 192 : at + 256]
                value = jnp.sum(jnp.where(row_hot, both, 0.0), axis=0, keepdims=True)
                parts.append(weight * value)
        high, low = halves(jnp.concatenate(parts, axis=0))
        here = (iota((tiles, 128), 0) == t).astype(BF16)
        return terms + mm(here, high, NT) + mm(here, low, NT)

    terms = jnp.zeros((tiles, 384), F32)
    ends = [0, 9 * tiles // 16, tiles]
    for stage, landing in enumerate((sum_x, sum_y)):
        target, size = axes[stage]
        sum_s[stage] = total
        copies = [send(sum_s.at[stage], landing.at[d - 1], target(d)) for d in range(1, size)]
        terms = lax.fori_loop(ends[stage], ends[stage + 1], term, terms)
        finish(copies)
        for d in range(1, size):
            total = total + landing[d - 1]
    total = jnp.where(group, jnp.broadcast_to(total, (8, 128)), 0.0)
    total = jnp.sum(total, axis=1, keepdims=True)
    norm, bend_a, bend_b, bend_c, bend_d = [total[q : q + 1, :] for q in range(5)]

    whole = norm + bend_a
    step = norm / whole
    rest = bend_a / whole
    norm_next = (norm / whole) * ((norm * bend_b - bend_a * bend_a) / whole)
    turn = norm_next / norm
    front = rest + turn
    bend_next = (
        front * front * whole
        - front * step * (2.0 * bend_a + bend_c + bend_b)
        + step * step * (bend_b + bend_d)
    )
    step_next = norm_next / bend_next
    alpha = step + step_next * front
    gamma = step * step_next

    match = iota((tiles, tiles), 0) == iota((tiles, tiles), 1)
    wide = jnp.broadcast_to(box_ref[...].astype(F32), (tiles, tiles))
    boxes = jnp.sum(jnp.where(match, wide, 0.0), axis=1, keepdims=True)
    terms = alpha * terms[:, 0:192] - gamma * terms[:, 192:384]
    terms = jnp.concatenate([terms, jnp.broadcast_to(boxes, (tiles, 64))], axis=1)
    by_ref[0] = terms
    copies = [send(by_ref.at[0], by_ref.at[d], to_y(d)) for d in range(1, yn)]
    for c in comps:
        field_ref[c] = alpha * search[c] - gamma * second[c]
    finish(copies)
    every = by_ref[...].reshape(yn * tiles, 256)
    per_y, per_x = xn * along, along
    box = every[:, 192:193]
    wanted = (my * per_y + iota((yn * tiles, 128), 1)).astype(F32)
    chosen = jnp.transpose((box == wanted).astype(F32))[:per_y].astype(BF16)
    high, low = halves(every)
    dense = mm(chosen, high) + mm(chosen, low)
    bxs_ref[...] = dense.reshape(xn, per_x, 256)
    copies = [send(bxs_ref.at[(mx + d) % xn], bxr_ref.at[d - 1], to_x(d)) for d in range(1, xn)]
    dense = bxs_ref[mx]
    finish(copies)
    for d in range(1, xn):
        dense = dense + bxr_ref[d - 1]
    for k in range(along):
        bzs_ref[k] = dense[k : k + 1, :]
    copies = [
        send(bzs_ref.at[(gy + d) % along], bzr_ref.at[d - 1], to_gy(d)) for d in range(1, along)
    ]
    dense = bzs_ref[gy]
    finish(copies)
    for d in range(1, along):
        dense = dense + bzr_ref[d - 1]
    grad_ref[...] = dense[:, 0:192]


def per_device(
    sizes,
    diag_blocks,
    edge_blocks,
    edge_mask,
    src_values,
    src_owner,
    src_node,
    src_count,
    surf_node,
    surf_param,
    tile_box,
):
    yn, xn, zn, cn = sizes
    tiles = tile_box.shape[0]
    rows = src_node.shape[0]
    vmem = pl.BlockSpec(memory_space=pltpu.VMEM)
    across, per_x = yn * xn, zn * cn
    copies = 2 * (across - 1) + 2 * (per_x - 1) + yn + xn - 2 + 8

    def buf(*shape):
        return pltpu.VMEM(shape, F32)

    operands = (
        src_count.reshape(1, 1),
        tile_box.reshape(1, tiles),
        diag_blocks,
        edge_blocks,
        edge_mask,
        src_values,
        src_owner.reshape(1, rows),
        src_node.reshape(1, rows),
        surf_node.reshape(tiles, 128),
        surf_param,
    )
    return pl.pallas_call(
        functools.partial(kernel, sizes),
        out_shape=(
            jax.ShapeDtypeStruct((3,) + diag_blocks.shape[1:], F32),
            jax.ShapeDtypeStruct((1, 192), F32),
        ),
        in_specs=[pl.BlockSpec(memory_space=pl.ANY)] * len(operands),
        out_specs=(vmem, vmem),
        scratch_shapes=[pltpu.VMEM(x.shape, x.dtype) for x in operands]
        + [
            buf(2, 8, rows),
            buf(across, 2, 128),
            buf(across, 2, 128),
            buf(2, 4, 8, 128),
            buf(2, 4, 8, 128),
            buf(2, 1, 128),
            buf(across - 1, 1, 128),
            buf(per_x - 1, 1, 128),
            buf(tiles, 64, 128),
            buf(yn, tiles, 256),
            buf(xn, per_x, 256),
            buf(xn - 1, per_x, 256),
            buf(per_x, 1, 256),
            buf(per_x - 1, 1, 256),
            pltpu.SemaphoreType.DMA((len(operands),)),
            pltpu.SemaphoreType.DMA((copies,)),
            pltpu.SemaphoreType.DMA((copies,)),
        ],
        compiler_params=pltpu.CompilerParams(
            collective_id=0, has_side_effects=True, vmem_limit_bytes=60 * 2**20
        ),
    )(*operands)


def solution(mesh):
    across, along = mesh.shape["gx"], mesh.shape["gy"]
    xn = 4 if across >= 16 else 2
    sizes = (across // xn, xn, along // 2, 2)
    return jax.shard_map(
        functools.partial(per_device, sizes),
        mesh=mesh,
        in_specs=(
            P(None, "gx", "gy"),
            P(None, None, "gx", "gy"),
            P(None, "gx", "gy"),
            P(None, ("gx", "gy")),
            P(("gx", "gy"), None),
            P(("gx", "gy")),
            P(("gx", "gy")),
            P(("gx", "gy")),
            P(None, ("gx", "gy")),
            P(("gx", "gy")),
        ),
        out_specs=(P(None, "gx", "gy"), P(("gx", "gy"), None)),
        check_vma=False,
    )
```

```python
import functools

import jax
import jax.numpy as jnp
from jax import lax
from jax.experimental import pallas as pl
from jax.experimental.pallas import tpu as pltpu
from jax.sharding import PartitionSpec as P

F32 = jnp.float32
BF16 = jnp.bfloat16
NT = (((1,), (1,)), ((), ()))


def halves(value):
    high = value.astype(BF16)
    low = (value - high.astype(F32)).astype(BF16)
    return high, low


def iota(shape, dim):
    return lax.broadcasted_iota(jnp.int32, shape, dim)


def mm(a, b, dims=(((1,), (0,)), ((), ()))):
    return lax.dot_general(a, b, dims, preferred_element_type=F32)


def kernel(
    sizes,
    count_hbm,
    box_hbm,
    diag_hbm,
    edge_hbm,
    mask_hbm,
    val_hbm,
    owner_hbm,
    node_hbm,
    surf_hbm,
    param_hbm,
    field_ref,
    grad_ref,
    count_ref,
    box_ref,
    diag_ref,
    edge_ref,
    mask_ref,
    val_ref,
    owner_ref,
    node_ref,
    surf_ref,
    param_ref,
    v8_ref,
    bin_ref,
    rx_ref,
    halo_s,
    halo_r,
    sum_s,
    sum_x,
    sum_y,
    weight_ref,
    id_ref,
    by_ref,
    bxs_ref,
    bxr_ref,
    bzs_ref,
    bzr_ref,
    load_sem,
    send_sem,
    recv_sem,
):
    yn, xn, zn, cn = sizes
    gx, gy = lax.axis_index("gx"), lax.axis_index("gy")
    my, mx = gx // xn, gx % xn

    def to_y(d):
        return (((my + d) % yn) * xn + mx, gy)

    def to_x(d):
        return (my * xn + (mx + d) % xn, gy)

    across, along = yn * xn, zn * cn

    def to_gx(d):
        return ((gx + d) % across, gy)

    def to_gy(d):
        return (gx, (gy + d) % along)

    around = [
        ((gx + 1) % (yn * xn), gy),
        ((gx + yn * xn - 1) % (yn * xn), gy),
        (gx, (gy + 1) % (zn * cn)),
        (gx, (gy + zn * cn - 1) % (zn * cn)),
    ]
    axes = [(to_gx, across), (to_gy, along)]

    moved = [
        (count_hbm, count_ref),
        (owner_hbm, owner_ref),
        (node_hbm, node_ref),
        (val_hbm, val_ref),
        (param_hbm, param_ref),
        (mask_hbm, mask_ref),
        (edge_hbm, edge_ref),
        (diag_hbm, diag_ref),
        (surf_hbm, surf_ref),
        (box_hbm, box_ref),
    ]
    loads = [
        pltpu.make_async_copy(src, dst, load_sem.at[n]) for n, (src, dst) in enumerate(moved)
    ]
    for copy in loads:
        copy.start()

    barrier = pltpu.get_barrier_semaphore()
    greeted = 0
    for target, size in axes:
        for d in range(1, size):
            pl.semaphore_signal(
                barrier, inc=1, device_id=target(d), device_id_type=pl.DeviceIdType.MESH
            )
            greeted += 1

    used = [0]

    def send(src, dst, target):
        slot = used[0]
        used[0] += 1
        copy = pltpu.make_async_remote_copy(
            src_ref=src,
            dst_ref=dst,
            send_sem=send_sem.at[slot],
            recv_sem=recv_sem.at[slot],
            device_id=target,
            device_id_type=pl.DeviceIdType.MESH,
        )
        copy.start()
        return copy

    def finish(copies):
        for copy in copies:
            copy.wait()

    owners = across
    for copy in loads[:4]:
        copy.wait()
    nodes = node_ref[...]
    lines = [val_ref[0:1, :], val_ref[2:3, :], val_ref[1:2, :], nodes.astype(F32)]
    for n, line in enumerate(lines):
        high, low = halves(line)
        at = n % 2 + 4 * (n // 2)
        v8_ref[at : at + 1, :] = high.astype(F32)
        v8_ref[at + 2 : at + 3, :] = low.astype(F32)
    rows = nodes.shape[1]
    live = iota((1, rows), 1) < count_ref[...]
    owner = jnp.where(live, owner_ref[...], -1)
    upper = (iota((128, 128), 0) <= iota((128, 128), 1)).astype(BF16)
    before = jnp.zeros((owners, 1), F32)
    binned = jnp.zeros((owners * 8, 128), F32)
    for b in range(rows // 128):
        cut = slice(128 * b, 128 * b + 128)
        hot = (iota((owners, 128), 0) == owner[:, cut]).astype(F32)
        order = mm(hot.astype(BF16), upper) + before
        before = before + jnp.sum(hot, axis=1, keepdims=True)
        rank = jnp.sum(hot * order, axis=0, keepdims=True) - 1.0
        place = ((iota((128, 128), 0) & 63).astype(F32) == rank).astype(BF16)
        spread = (hot[:, None, :] * v8_ref[:, cut][None, :, :]).reshape(owners * 8, 128)
        binned = binned + mm(spread.astype(BF16), place, NT)
    binned = binned.reshape(owners, 8, 128)
    near = binned[:, 0:2, :] + binned[:, 2:4, :]
    far = binned[:, 4:6, :] + binned[:, 6:8, :]
    bin_ref[...] = jnp.where(iota((owners, 2, 128), 2) < 64, near, far)

    pl.semaphore_wait(barrier, greeted)
    copies = [
        send(bin_ref.at[(gx + d) % across], rx_ref.at[d], to_gx(d)) for d in range(1, across)
    ]
    rx_ref[0] = bin_ref[gx]

    loads[9].wait()
    tiles = surf_ref.shape[0]
    ids = box_ref[...].astype(F32)
    ids = jnp.concatenate([ids, jnp.zeros((1, 128 - tiles), F32)], axis=1)
    id_ref[0] = ids
    id_copies = [send(id_ref.at[0], id_ref.at[d], to_y(d)) for d in range(1, yn)]

    def bern(coord, index):
        other = 1.0 - coord
        return jnp.where(
            index == 0,
            other * other * other,
            jnp.where(
                index == 1,
                3.0 * coord * other * other,
                jnp.where(index == 2, 3.0 * coord * coord * other, coord * coord * coord),
            ),
        )

    line = iota((64, 128), 0)

    def weights(t, carry):
        cut = pl.ds(pl.multiple_of(t * 128, 128), 128)
        first = bern(param_ref[0:1, cut], line // 16)
        second = bern(param_ref[1:2, cut], (line // 4) % 4)
        third = bern(param_ref[2:3, cut], line % 4)
        weight_ref[t] = first * second * third
        return carry

    loads[4].wait()
    lax.fori_loop(0, tiles, weights, 0)

    for copy in loads[5:9]:
        copy.wait()
    for d in range(4):
        keep = mask_ref[d].astype(F32)
        for n in range(9):
            edge_ref[d, n] = edge_ref[d, n] * keep

    finish(copies)
    finish(id_copies)
    per_y, per_x = xn * along, along
    lane = iota((1, 128), 1)
    half = tiles // 2
    id_all, id_low, id_high = ids, jnp.where(lane < half, ids, 0.0), None
    id_high = pltpu.roll(jnp.where(lane < half, 0.0, ids), 128 - half, 1)
    for d in range(1, yn):
        ids = id_ref[d]
        id_all = id_all + pltpu.roll(ids, tiles * d, 1)
        id_low = id_low + pltpu.roll(jnp.where(lane < half, ids, 0.0), half * d, 1)
        turned = jnp.where(lane < half, 0.0, ids)
        id_high = id_high + pltpu.roll(turned, (128 + half * (d - 1)) % 128, 1)

    def chosen(ids, width):
        wanted = (my * per_y + iota((per_y, 128), 0)).astype(F32)
        return (wanted == ids).astype(F32)[:, :width].astype(BF16)

    pick_all = chosen(id_all, yn * tiles)
    pick_low = chosen(id_low, yn * half)
    pick_high = chosen(id_high, yn * half)

    left_half = iota((2, 128), 1) < 64

    def scatter(t, total):
        lefts, cols = [], []
        for k in range(2):
            one, two = rx_ref[4 * t + 2 * k], rx_ref[4 * t + 2 * k + 1]
            near = jnp.where(left_half, one, pltpu.roll(two, 64, 1))
            far = jnp.where(left_half, pltpu.roll(one, 64, 1), two)
            node = far[1:2, :].astype(jnp.int32)
            row_hot = iota((64, 128), 0) == (node >> 7)
            cols.append((iota((128, 128), 0) == (node & 127)).astype(BF16))
            values = [near[0:1, :], far[0:1, :], near[1:2, :]]
            left = jnp.concatenate([jnp.where(row_hot, v, 0.0) for v in values], axis=0)
            lefts.append(jnp.concatenate(halves(left), axis=0))
        return total + mm(jnp.concatenate(lefts, axis=1), jnp.concatenate(cols, axis=1), NT)

    load = lax.fori_loop(0, owners // 4, scatter, jnp.zeros((384, 128), F32))
    load = load[0:192] + load[192:384]
    comps = range(3)
    residual = [load[64 * c : 64 * c + 64] for c in comps]

    row_id, lane_id = iota((64, 128), 0), iota((64, 128), 1)
    same = row_id == lane_id
    zero_rows = jnp.zeros((5, 128), F32)

    def operator(field, h):
        def product(d, part=slice(0, 64)):
            return [
                edge_ref[d, c, part] * field[0][part]
                + edge_ref[d, 3 + c, part] * field[1][part]
                + edge_ref[d, 6 + c, part] * field[2][part]
                for c in comps
            ]

        def column(value, lane):
            wide = jnp.broadcast_to(value[:, lane : lane + 1], (64, 128))
            return jnp.sum(jnp.where(same, wide, 0.0), axis=0, keepdims=True)

        def give(k, lines):
            halo_s[h, k] = jnp.concatenate(lines + [zero_rows], axis=0)
            return send(halo_s.at[h, k], halo_r.at[h, k], around[k])

        copies = [
            give(0, [line[7:8, :] for line in product(0, slice(56, 64))]),
            give(1, [line[0:1, :] for line in product(1, slice(0, 8))]),
        ]
        up_y, low_y = product(2), product(3)
        copies.append(give(2, [column(up_y[c], 127) for c in comps]))
        copies.append(give(3, [column(low_y[c], 0) for c in comps]))
        up_x, low_x = product(0), product(1)
        inner = [
            sum(diag_ref[3 * k + c] * field[k] for k in comps if k != c)
            + jnp.where(row_id == 0, 0.0, pltpu.roll(up_x[c], 1, 0))
            + jnp.where(row_id == 63, 0.0, pltpu.roll(low_x[c], 63, 0))
            + jnp.where(lane_id == 0, 0.0, pltpu.roll(up_y[c], 1, 1))
            + jnp.where(lane_id == 127, 0.0, pltpu.roll(low_y[c], 127, 1))
            for c in comps
        ]
        finish(copies)
        there = [gx > 0, gx < yn * xn - 1, gy > 0, gy < zn * cn - 1]
        got = [halo_r[h, k] * there[k].astype(F32) for k in range(4)]

        def upright(row):
            wide = jnp.broadcast_to(row, (64, 128))
            return jnp.sum(jnp.where(same, wide, 0.0), axis=1, keepdims=True)

        return [
            inner[c]
            + jnp.where(row_id == 0, got[0][c : c + 1, :], 0.0)
            + jnp.where(row_id == 63, got[1][c : c + 1, :], 0.0)
            + jnp.where(lane_id == 0, upright(got[2][c : c + 1, :]), 0.0)
            + jnp.where(lane_id == 127, upright(got[3][c : c + 1, :]), 0.0)
            for c in comps
        ]

    def partial(a, b):
        return jnp.sum(a[0] * b[0] + a[1] * b[1] + a[2] * b[2], axis=0, keepdims=True)

    scale = [diag_ref[0], diag_ref[4], diag_ref[8]]
    search = [residual[c] / scale[c] for c in comps]
    other = operator(search, 0)
    second = [other[c] / scale[c] for c in comps]
    third = operator(second, 1)
    lines = [
        partial(search, residual),
        partial(search, other),
        partial(second, other),
        partial(search, third),
        partial(second, third),
    ]
    total = jnp.concatenate(lines + [jnp.zeros((8 - len(lines), 128), F32)], axis=0)
    for shift in (64, 32, 16):
        total = total + pltpu.roll(total, shift, 1)
    group = iota((8, 128), 1) // 16 == iota((8, 128), 0)
    total = jnp.sum(jnp.where(group, total, 0.0), axis=0, keepdims=True)

    pieces = halves(jnp.concatenate(search, axis=0)) + halves(jnp.concatenate(second, axis=0))
    stacked = jnp.concatenate(pieces, axis=0)

    def term(t, terms):
        nodes = [surf_ref[pl.ds(2 * t + k, 1), :] for k in range(2)]
        cols = [(iota((128, 128), 0) == (node & 127)).astype(BF16) for node in nodes]
        picked = mm(stacked, jnp.concatenate(cols, axis=1))
        tops, bottoms, heres = [], [], []
        for k in range(2):
            row_hot = iota((64, 128), 0) == (nodes[k] >> 7)
            weight = weight_ref[2 * t + k]
            parts = []
            for first in (0, 384):
                for c in comps:
                    at = first + 64 * c
                    side = picked[:, 128 * k : 128 * k + 128]
                    both = side[at : at + 64] + side[at + 192 : at + 256]
                    value = jnp.sum(jnp.where(row_hot, both, 0.0), axis=0, keepdims=True)
                    parts.append(weight * value)
            high, low = halves(jnp.concatenate(parts, axis=0))
            tops.append(high)
            bottoms.append(low)
            heres.append((iota((tiles, 128), 0) == 2 * t + k).astype(BF16))
        here = jnp.concatenate(heres, axis=1)
        high, low = jnp.concatenate(tops, axis=1), jnp.concatenate(bottoms, axis=1)
        return terms + mm(here, high, NT) + mm(here, low, NT)

    terms = jnp.zeros((tiles, 384), F32)
    ends = [0, 5 * tiles // 16, tiles // 2]
    for stage, landing in enumerate((sum_x, sum_y)):
        target, size = axes[stage]
        sum_s[stage] = total
        copies = [send(sum_s.at[stage], landing.at[d - 1], target(d)) for d in range(1, size)]
        terms = lax.fori_loop(ends[stage], ends[stage + 1], term, terms)
        finish(copies)
        for d in range(1, size):
            total = total + landing[d - 1]
    total = jnp.where(group, jnp.broadcast_to(total, (8, 128)), 0.0)
    total = jnp.sum(total, axis=1, keepdims=True)
    norm, bend_a, bend_b, bend_c, bend_d = [total[q : q + 1, :] for q in range(5)]

    whole = norm + bend_a
    step = norm / whole
    rest = bend_a / whole
    norm_next = (norm / whole) * ((norm * bend_b - bend_a * bend_a) / whole)
    turn = norm_next / norm
    front = rest + turn
    bend_next = (
        front * front * whole
        - front * step * (2.0 * bend_a + bend_c + bend_b)
        + step * step * (bend_b + bend_d)
    )
    step_next = norm_next / bend_next
    alpha = step + step_next * front
    gamma = step * step_next

    terms = alpha * terms[:, 0:192] - gamma * terms[:, 192:384]
    by_ref[0, 0:tiles, :] = terms[:, 0:128]
    by_ref[0, tiles:, :] = jnp.concatenate([terms[:half, 128:192], terms[half:, 128:192]], axis=1)
    copies = [send(by_ref.at[0], by_ref.at[d], to_y(d)) for d in range(1, yn)]
    for c in comps:
        field_ref[c] = alpha * search[c] - gamma * second[c]
    finish(copies)
    high, low = halves(by_ref[:, 0:tiles, :].reshape(yn * tiles, 128))
    dense = mm(pick_all, high) + mm(pick_all, low)
    high, low = halves(by_ref[:, tiles:, :].reshape(yn * half, 128))
    near = mm(pick_low, high) + mm(pick_low, low)
    far = mm(pick_high, high) + mm(pick_high, low)
    near = jnp.where(iota(near.shape, 1) < 64, near + pltpu.roll(far, 64, 1), 0.0)
    dense = jnp.concatenate([dense, near], axis=1)
    bxs_ref[...] = dense.reshape(xn, per_x, 256)
    copies = [send(bxs_ref.at[(mx + d) % xn], bxr_ref.at[d - 1], to_x(d)) for d in range(1, xn)]
    dense = bxs_ref[mx]
    finish(copies)
    for d in range(1, xn):
        dense = dense + bxr_ref[d - 1]
    for k in range(along):
        bzs_ref[k] = dense[k : k + 1, :]
    copies = [
        send(bzs_ref.at[(gy + d) % along], bzr_ref.at[d - 1], to_gy(d)) for d in range(1, along)
    ]
    dense = bzs_ref[gy]
    finish(copies)
    for d in range(1, along):
        dense = dense + bzr_ref[d - 1]
    grad_ref[...] = dense[:, 0:192]


def per_device(
    sizes,
    diag_blocks,
    edge_blocks,
    edge_mask,
    src_values,
    src_owner,
    src_node,
    src_count,
    surf_node,
    surf_param,
    tile_box,
):
    yn, xn, zn, cn = sizes
    tiles = tile_box.shape[0]
    rows = src_node.shape[0]
    vmem = pl.BlockSpec(memory_space=pltpu.VMEM)
    across, per_x = yn * xn, zn * cn
    copies = 2 * (across - 1) + 2 * (per_x - 1) + 2 * (yn - 1) + xn - 1 + 8

    def buf(*shape):
        return pltpu.VMEM(shape, F32)

    operands = (
        src_count.reshape(1, 1),
        tile_box.reshape(1, tiles),
        diag_blocks,
        edge_blocks,
        edge_mask,
        src_values,
        src_owner.reshape(1, rows),
        src_node.reshape(1, rows),
        surf_node.reshape(tiles, 128),
        surf_param,
    )
    return pl.pallas_call(
        functools.partial(kernel, sizes),
        out_shape=(
            jax.ShapeDtypeStruct((3,) + diag_blocks.shape[1:], F32),
            jax.ShapeDtypeStruct((1, 192), F32),
        ),
        in_specs=[pl.BlockSpec(memory_space=pl.ANY)] * len(operands),
        out_specs=(vmem, vmem),
        scratch_shapes=[pltpu.VMEM(x.shape, x.dtype) for x in operands]
        + [
            buf(8, rows),
            buf(across, 2, 128),
            buf(across, 2, 128),
            buf(2, 4, 8, 128),
            buf(2, 4, 8, 128),
            buf(2, 1, 128),
            buf(across - 1, 1, 128),
            buf(per_x - 1, 1, 128),
            buf(tiles, 64, 128),
            buf(yn, 1, 128),
            buf(yn, tiles * 3 // 2, 128),
            buf(xn, per_x, 256),
            buf(xn - 1, per_x, 256),
            buf(per_x, 1, 256),
            buf(per_x - 1, 1, 256),
            pltpu.SemaphoreType.DMA((len(operands),)),
            pltpu.SemaphoreType.DMA((copies,)),
            pltpu.SemaphoreType.DMA((copies,)),
        ],
        compiler_params=pltpu.CompilerParams(
            collective_id=0, has_side_effects=True, vmem_limit_bytes=60 * 2**20
        ),
    )(*operands)


def solution(mesh):
    across, along = mesh.shape["gx"], mesh.shape["gy"]
    xn = 4 if across >= 16 else 2
    sizes = (across // xn, xn, along // 2, 2)
    return jax.shard_map(
        functools.partial(per_device, sizes),
        mesh=mesh,
        in_specs=(
            P(None, "gx", "gy"),
            P(None, None, "gx", "gy"),
            P(None, "gx", "gy"),
            P(None, ("gx", "gy")),
            P(("gx", "gy"), None),
            P(("gx", "gy")),
            P(("gx", "gy")),
            P(("gx", "gy")),
            P(None, ("gx", "gy")),
            P(("gx", "gy")),
        ),
        out_specs=(P(None, "gx", "gy"), P(("gx", "gy"), None)),
        check_vma=False,
    )
```

```python
import functools

import jax
import jax.numpy as jnp
from jax import lax
from jax.experimental import pallas as pl
from jax.experimental.pallas import tpu as pltpu
from jax.sharding import PartitionSpec as P

F32 = jnp.float32
BF16 = jnp.bfloat16
NT = (((1,), (1,)), ((), ()))


def halves(value):
    high = value.astype(BF16)
    low = (value - high.astype(F32)).astype(BF16)
    return high, low


def iota(shape, dim):
    return lax.broadcasted_iota(jnp.int32, shape, dim)


def far_first(size):
    return sorted(range(1, size), key=lambda d: abs(2 * d - size))


def mm(a, b, dims=(((1,), (0,)), ((), ()))):
    return lax.dot_general(a, b, dims, preferred_element_type=F32)


def kernel(
    sizes,
    count_hbm,
    box_hbm,
    diag_hbm,
    edge_hbm,
    mask_hbm,
    val_hbm,
    owner_hbm,
    node_hbm,
    surf_hbm,
    param_hbm,
    field_ref,
    grad_ref,
    count_ref,
    box_ref,
    diag_ref,
    edge_ref,
    mask_ref,
    val_ref,
    owner_ref,
    node_ref,
    surf_ref,
    param_ref,
    v8_ref,
    bin_ref,
    rx_ref,
    halo_s,
    halo_r,
    sum_s,
    sum_x,
    sum_y,
    weight_ref,
    inv_ref,
    id_ref,
    by_ref,
    bxs_ref,
    bxr_ref,
    bzs_ref,
    bzr_ref,
    load_sem,
    send_sem,
    recv_sem,
):
    yn, xn, zn, cn = sizes
    gx, gy = lax.axis_index("gx"), lax.axis_index("gy")
    my, mx = gx // xn, gx % xn

    def to_y(d):
        return (((my + d) % yn) * xn + mx, gy)

    def to_x(d):
        return (my * xn + (mx + d) % xn, gy)

    across, along = yn * xn, zn * cn

    def to_gx(d):
        return ((gx + d) % across, gy)

    def to_gy(d):
        return (gx, (gy + d) % along)

    around = [
        ((gx + 1) % (yn * xn), gy),
        ((gx + yn * xn - 1) % (yn * xn), gy),
        (gx, (gy + 1) % (zn * cn)),
        (gx, (gy + zn * cn - 1) % (zn * cn)),
    ]
    axes = [(to_gx, across), (to_gy, along)]

    moved = [
        (count_hbm, count_ref),
        (owner_hbm, owner_ref),
        (node_hbm, node_ref),
        (val_hbm, val_ref),
        (param_hbm, param_ref),
        (mask_hbm, mask_ref),
        (edge_hbm, edge_ref),
        (diag_hbm, diag_ref),
        (surf_hbm, surf_ref),
        (box_hbm, box_ref),
    ]
    loads = [
        pltpu.make_async_copy(src, dst, load_sem.at[n]) for n, (src, dst) in enumerate(moved)
    ]
    for copy in loads:
        copy.start()

    barrier = pltpu.get_barrier_semaphore()
    greeted = 0
    for target, size in axes:
        for d in range(1, size):
            pl.semaphore_signal(
                barrier, inc=1, device_id=target(d), device_id_type=pl.DeviceIdType.MESH
            )
            greeted += 1

    used = [0]

    def send(src, dst, target):
        slot = used[0]
        used[0] += 1
        copy = pltpu.make_async_remote_copy(
            src_ref=src,
            dst_ref=dst,
            send_sem=send_sem.at[slot],
            recv_sem=recv_sem.at[slot],
            device_id=target,
            device_id_type=pl.DeviceIdType.MESH,
        )
        copy.start()
        return copy

    def finish(copies):
        for copy in copies:
            copy.wait()

    owners = across
    for copy in loads[:4]:
        copy.wait()
    nodes = node_ref[...]
    lines = [val_ref[0:1, :], val_ref[2:3, :], val_ref[1:2, :], nodes.astype(F32)]
    for n, line in enumerate(lines):
        high, low = halves(line)
        at = n % 2 + 4 * (n // 2)
        v8_ref[at : at + 1, :] = high.astype(F32)
        v8_ref[at + 2 : at + 3, :] = low.astype(F32)
    rows = nodes.shape[1]
    live = iota((1, rows), 1) < count_ref[...]
    owner = jnp.where(live, owner_ref[...], -1)
    upper = (iota((128, 128), 0) <= iota((128, 128), 1)).astype(BF16)
    before = jnp.zeros((owners, 1), F32)
    binned = jnp.zeros((owners * 8, 128), F32)
    for b in range(rows // 128):
        cut = slice(128 * b, 128 * b + 128)
        hot = (iota((owners, 128), 0) == owner[:, cut]).astype(F32)
        order = mm(hot.astype(BF16), upper) + before
        before = before + jnp.sum(hot, axis=1, keepdims=True)
        rank = jnp.sum(hot * order, axis=0, keepdims=True) - 1.0
        place = ((iota((128, 128), 0) & 63).astype(F32) == rank).astype(BF16)
        spread = (hot[:, None, :] * v8_ref[:, cut][None, :, :]).reshape(owners * 8, 128)
        binned = binned + mm(spread.astype(BF16), place, NT)
    binned = binned.reshape(owners, 8, 128)
    near = binned[:, 0:2, :] + binned[:, 2:4, :]
    far = binned[:, 4:6, :] + binned[:, 6:8, :]
    bin_ref[...] = jnp.where(iota((owners, 2, 128), 2) < 64, near, far)

    pl.semaphore_wait(barrier, greeted)
    copies = [
        send(bin_ref.at[(gx + d) % across], rx_ref.at[d], to_gx(d)) for d in far_first(across)
    ]
    rx_ref[0] = bin_ref[gx]

    loads[9].wait()
    tiles = surf_ref.shape[0]
    ids = box_ref[...].astype(F32)
    ids = jnp.concatenate([ids, jnp.zeros((1, 128 - tiles), F32)], axis=1)
    id_ref[0] = ids
    id_copies = [send(id_ref.at[0], id_ref.at[d], to_y(d)) for d in far_first(yn)]

    def bern(coord, index):
        other = 1.0 - coord
        return jnp.where(
            index == 0,
            other * other * other,
            jnp.where(
                index == 1,
                3.0 * coord * other * other,
                jnp.where(index == 2, 3.0 * coord * coord * other, coord * coord * coord),
            ),
        )

    line = iota((64, 128), 0)

    def weights(t, carry):
        cut = pl.ds(pl.multiple_of(t * 128, 128), 128)
        first = bern(param_ref[0:1, cut], line // 16)
        second = bern(param_ref[1:2, cut], (line // 4) % 4)
        third = bern(param_ref[2:3, cut], line % 4)
        weight_ref[t] = first * second * third
        return carry

    loads[4].wait()
    lax.fori_loop(0, tiles, weights, 0)

    for copy in loads[5:9]:
        copy.wait()
    for n in range(3):
        inv_ref[n] = 1.0 / diag_ref[4 * n]
    for d in range(4):
        keep = mask_ref[d].astype(F32)
        for n in range(9):
            edge_ref[d, n] = edge_ref[d, n] * keep

    finish(copies)
    left_half = iota((2, 128), 1) < 64

    def scatter(t, total):
        lefts, cols = [], []
        for k in range(2):
            one, two = rx_ref[4 * t + 2 * k], rx_ref[4 * t + 2 * k + 1]
            near = jnp.where(left_half, one, pltpu.roll(two, 64, 1))
            far = jnp.where(left_half, pltpu.roll(one, 64, 1), two)
            node = far[1:2, :].astype(jnp.int32)
            row_hot = iota((64, 128), 0) == (node >> 7)
            cols.append((iota((128, 128), 0) == (node & 127)).astype(BF16))
            values = [near[0:1, :], far[0:1, :], near[1:2, :]]
            left = jnp.concatenate([jnp.where(row_hot, v, 0.0) for v in values], axis=0)
            lefts.append(jnp.concatenate(halves(left), axis=0))
        return total + mm(jnp.concatenate(lefts, axis=1), jnp.concatenate(cols, axis=1), NT)

    load = lax.fori_loop(0, owners // 4, scatter, jnp.zeros((384, 128), F32))
    load = load[0:192] + load[192:384]
    comps = range(3)
    residual = [load[64 * c : 64 * c + 64] for c in comps]

    row_id, lane_id = iota((64, 128), 0), iota((64, 128), 1)
    same = row_id == lane_id
    zero_rows = jnp.zeros((5, 128), F32)

    def operator(field, h):
        def product(d, part=slice(0, 64)):
            return [
                edge_ref[d, c, part] * field[0][part]
                + edge_ref[d, 3 + c, part] * field[1][part]
                + edge_ref[d, 6 + c, part] * field[2][part]
                for c in comps
            ]

        def column(value, lane):
            wide = jnp.broadcast_to(value[:, lane : lane + 1], (64, 128))
            return jnp.sum(jnp.where(same, wide, 0.0), axis=0, keepdims=True)

        def give(k, lines):
            halo_s[h, k] = jnp.concatenate(lines + [zero_rows], axis=0)
            return send(halo_s.at[h, k], halo_r.at[h, k], around[k])

        copies = [
            give(0, [line[7:8, :] for line in product(0, slice(56, 64))]),
            give(1, [line[0:1, :] for line in product(1, slice(0, 8))]),
        ]
        up_y, low_y = product(2), product(3)
        copies.append(give(2, [column(up_y[c], 127) for c in comps]))
        copies.append(give(3, [column(low_y[c], 0) for c in comps]))
        up_x, low_x = product(0), product(1)
        inner = [
            sum(diag_ref[3 * k + c] * field[k] for k in comps if k != c)
            + jnp.where(row_id == 0, 0.0, pltpu.roll(up_x[c], 1, 0))
            + jnp.where(row_id == 63, 0.0, pltpu.roll(low_x[c], 63, 0))
            + jnp.where(lane_id == 0, 0.0, pltpu.roll(up_y[c], 1, 1))
            + jnp.where(lane_id == 127, 0.0, pltpu.roll(low_y[c], 127, 1))
            for c in comps
        ]
        finish(copies)
        there = [gx > 0, gx < yn * xn - 1, gy > 0, gy < zn * cn - 1]
        got = [halo_r[h, k] * there[k].astype(F32) for k in range(4)]

        def upright(row):
            wide = jnp.broadcast_to(row, (64, 128))
            return jnp.sum(jnp.where(same, wide, 0.0), axis=1, keepdims=True)

        return [
            inner[c]
            + jnp.where(row_id == 0, got[0][c : c + 1, :], 0.0)
            + jnp.where(row_id == 63, got[1][c : c + 1, :], 0.0)
            + jnp.where(lane_id == 0, upright(got[2][c : c + 1, :]), 0.0)
            + jnp.where(lane_id == 127, upright(got[3][c : c + 1, :]), 0.0)
            for c in comps
        ]

    def partial(a, b):
        return jnp.sum(a[0] * b[0] + a[1] * b[1] + a[2] * b[2], axis=0, keepdims=True)

    search = [residual[c] * inv_ref[c] for c in comps]
    other = operator(search, 0)
    second = [other[c] * inv_ref[c] for c in comps]
    third = operator(second, 1)
    lines = [
        partial(search, residual),
        partial(search, other),
        partial(second, other),
        partial(search, third),
        partial(second, third),
    ]
    total = jnp.concatenate(lines + [jnp.zeros((8 - len(lines), 128), F32)], axis=0)
    for shift in (64, 32, 16):
        total = total + pltpu.roll(total, shift, 1)
    group = iota((8, 128), 1) // 16 == iota((8, 128), 0)
    total = jnp.sum(jnp.where(group, total, 0.0), axis=0, keepdims=True)

    pieces = halves(jnp.concatenate(search, axis=0)) + halves(jnp.concatenate(second, axis=0))
    stacked = jnp.concatenate(pieces, axis=0)

    def term(t, terms):
        nodes = [surf_ref[pl.ds(2 * t + k, 1), :] for k in range(2)]
        cols = [(iota((128, 128), 0) == (node & 127)).astype(BF16) for node in nodes]
        picked = mm(stacked, jnp.concatenate(cols, axis=1))
        tops, bottoms, heres = [], [], []
        for k in range(2):
            row_hot = iota((64, 128), 0) == (nodes[k] >> 7)
            weight = weight_ref[2 * t + k]
            parts = []
            for first in (0, 384):
                for c in comps:
                    at = first + 64 * c
                    side = picked[:, 128 * k : 128 * k + 128]
                    both = side[at : at + 64] + side[at + 192 : at + 256]
                    value = jnp.sum(jnp.where(row_hot, both, 0.0), axis=0, keepdims=True)
                    parts.append(weight * value)
            high, low = halves(jnp.concatenate(parts, axis=0))
            tops.append(high)
            bottoms.append(low)
            heres.append((iota((tiles, 128), 0) == 2 * t + k).astype(BF16))
        here = jnp.concatenate(heres, axis=1)
        high, low = jnp.concatenate(tops, axis=1), jnp.concatenate(bottoms, axis=1)
        return terms + mm(here, high, NT) + mm(here, low, NT)

    half = tiles // 2
    per_y, per_x = xn * along, along

    def box_picks():
        finish(id_copies)
        own = id_ref[0]
        lane = iota((1, 128), 1)
        id_all, id_low = own, jnp.where(lane < half, own, 0.0)
        id_high = pltpu.roll(jnp.where(lane < half, 0.0, own), 128 - half, 1)
        for d in range(1, yn):
            line = id_ref[d]
            id_all = id_all + pltpu.roll(line, tiles * d, 1)
            id_low = id_low + pltpu.roll(jnp.where(lane < half, line, 0.0), half * d, 1)
            turned = jnp.where(lane < half, 0.0, line)
            id_high = id_high + pltpu.roll(turned, (128 + half * (d - 1)) % 128, 1)

        def chosen(ids, width):
            wanted = (my * per_y + iota((per_y, 128), 0)).astype(F32)
            return (wanted == ids).astype(F32)[:, :width].astype(BF16)

        return (
            chosen(id_all, yn * tiles),
            chosen(id_low, yn * half),
            chosen(id_high, yn * half),
        )

    terms = jnp.zeros((tiles, 384), F32)
    ends = [0, 5 * tiles // 16, tiles // 2]
    for stage, landing in enumerate((sum_x, sum_y)):
        target, size = axes[stage]
        sum_s[stage] = total
        copies = [send(sum_s.at[stage], landing.at[d - 1], target(d)) for d in far_first(size)]
        if stage == 1:
            pick_all, pick_low, pick_high = box_picks()
        terms = lax.fori_loop(ends[stage], ends[stage + 1], term, terms)
        finish(copies)
        for d in range(1, size):
            total = total + landing[d - 1]
    total = jnp.where(group, jnp.broadcast_to(total, (8, 128)), 0.0)
    total = jnp.sum(total, axis=1, keepdims=True)
    norm, bend_a, bend_b, bend_c, bend_d = [total[q : q + 1, :] for q in range(5)]

    whole = norm + bend_a
    step = norm / whole
    rest = bend_a / whole
    norm_next = (norm / whole) * ((norm * bend_b - bend_a * bend_a) / whole)
    turn = norm_next / norm
    front = rest + turn
    bend_next = (
        front * front * whole
        - front * step * (2.0 * bend_a + bend_c + bend_b)
        + step * step * (bend_b + bend_d)
    )
    step_next = norm_next / bend_next
    alpha = step + step_next * front
    gamma = step * step_next

    terms = alpha * terms[:, 0:192] - gamma * terms[:, 192:384]
    by_ref[0, 0:tiles, :] = terms[:, 0:128]
    by_ref[0, tiles:, :] = jnp.concatenate([terms[:half, 128:192], terms[half:, 128:192]], axis=1)
    copies = [send(by_ref.at[0], by_ref.at[d], to_y(d)) for d in far_first(yn)]
    for c in comps:
        field_ref[c] = alpha * search[c] - gamma * second[c]
    finish(copies)
    high, low = halves(by_ref[:, 0:tiles, :].reshape(yn * tiles, 128))
    dense = mm(pick_all, high) + mm(pick_all, low)
    high, low = halves(by_ref[:, tiles:, :].reshape(yn * half, 128))
    near = mm(pick_low, high) + mm(pick_low, low)
    far = mm(pick_high, high) + mm(pick_high, low)
    near = jnp.where(iota(near.shape, 1) < 64, near + pltpu.roll(far, 64, 1), 0.0)
    dense = jnp.concatenate([dense, near], axis=1)
    bxs_ref[...] = dense.reshape(xn, per_x, 256)
    copies = [send(bxs_ref.at[(mx + d) % xn], bxr_ref.at[d - 1], to_x(d)) for d in far_first(xn)]
    dense = bxs_ref[mx]
    finish(copies)
    for d in range(1, xn):
        dense = dense + bxr_ref[d - 1]
    for k in range(along):
        bzs_ref[k] = dense[k : k + 1, :]
    copies = [
        send(bzs_ref.at[(gy + d) % along], bzr_ref.at[d - 1], to_gy(d)) for d in far_first(along)
    ]
    dense = bzs_ref[gy]
    finish(copies)
    for d in range(1, along):
        dense = dense + bzr_ref[d - 1]
    grad_ref[...] = dense[:, 0:192]


def per_device(
    sizes,
    diag_blocks,
    edge_blocks,
    edge_mask,
    src_values,
    src_owner,
    src_node,
    src_count,
    surf_node,
    surf_param,
    tile_box,
):
    yn, xn, zn, cn = sizes
    tiles = tile_box.shape[0]
    rows = src_node.shape[0]
    vmem = pl.BlockSpec(memory_space=pltpu.VMEM)
    across, per_x = yn * xn, zn * cn
    copies = 2 * (across - 1) + 2 * (per_x - 1) + 2 * (yn - 1) + xn - 1 + 8

    def buf(*shape):
        return pltpu.VMEM(shape, F32)

    operands = (
        src_count.reshape(1, 1),
        tile_box.reshape(1, tiles),
        diag_blocks,
        edge_blocks,
        edge_mask,
        src_values,
        src_owner.reshape(1, rows),
        src_node.reshape(1, rows),
        surf_node.reshape(tiles, 128),
        surf_param,
    )
    return pl.pallas_call(
        functools.partial(kernel, sizes),
        out_shape=(
            jax.ShapeDtypeStruct((3,) + diag_blocks.shape[1:], F32),
            jax.ShapeDtypeStruct((1, 192), F32),
        ),
        in_specs=[pl.BlockSpec(memory_space=pl.ANY)] * len(operands),
        out_specs=(vmem, vmem),
        scratch_shapes=[pltpu.VMEM(x.shape, x.dtype) for x in operands]
        + [
            buf(8, rows),
            buf(across, 2, 128),
            buf(across, 2, 128),
            buf(2, 4, 8, 128),
            buf(2, 4, 8, 128),
            buf(2, 1, 128),
            buf(across - 1, 1, 128),
            buf(per_x - 1, 1, 128),
            buf(tiles, 64, 128),
            buf(3, 64, 128),
            buf(yn, 1, 128),
            buf(yn, tiles * 3 // 2, 128),
            buf(xn, per_x, 256),
            buf(xn - 1, per_x, 256),
            buf(per_x, 1, 256),
            buf(per_x - 1, 1, 256),
            pltpu.SemaphoreType.DMA((len(operands),)),
            pltpu.SemaphoreType.DMA((copies,)),
            pltpu.SemaphoreType.DMA((copies,)),
        ],
        compiler_params=pltpu.CompilerParams(
            collective_id=0, has_side_effects=True, vmem_limit_bytes=60 * 2**20
        ),
    )(*operands)


def solution(mesh):
    across, along = mesh.shape["gx"], mesh.shape["gy"]
    xn = 4 if across >= 16 else 2
    sizes = (across // xn, xn, along // 2, 2)
    return jax.shard_map(
        functools.partial(per_device, sizes),
        mesh=mesh,
        in_specs=(
            P(None, "gx", "gy"),
            P(None, None, "gx", "gy"),
            P(None, "gx", "gy"),
            P(None, ("gx", "gy")),
            P(("gx", "gy"), None),
            P(("gx", "gy")),
            P(("gx", "gy")),
            P(("gx", "gy")),
            P(None, ("gx", "gy")),
            P(("gx", "gy")),
        ),
        out_specs=(P(None, "gx", "gy"), P(("gx", "gy"), None)),
        check_vma=False,
    )
```

```python
import functools

import jax
import jax.numpy as jnp
from jax import lax
from jax.experimental import pallas as pl
from jax.experimental.pallas import tpu as pltpu
from jax.sharding import PartitionSpec as P

F32 = jnp.float32
BF16 = jnp.bfloat16
NT = (((1,), (1,)), ((), ()))


def halves(value):
    high = value.astype(BF16)
    low = (value - high.astype(F32)).astype(BF16)
    return high, low


def iota(shape, dim):
    return lax.broadcasted_iota(jnp.int32, shape, dim)


def far_first(size):
    return sorted(range(1, size), key=lambda d: abs(2 * d - size))


def mm(a, b, dims=(((1,), (0,)), ((), ()))):
    return lax.dot_general(a, b, dims, preferred_element_type=F32)


def kernel(
    sizes,
    count_hbm,
    box_hbm,
    diag_hbm,
    edge_hbm,
    mask_hbm,
    val_hbm,
    owner_hbm,
    node_hbm,
    surf_hbm,
    param_hbm,
    field_ref,
    grad_ref,
    count_ref,
    box_ref,
    diag_ref,
    edge_ref,
    mask_ref,
    val_ref,
    owner_ref,
    node_ref,
    surf_ref,
    param_ref,
    v8_ref,
    bin_ref,
    rx_ref,
    halo_s,
    halo_r,
    sum_s,
    sum_x,
    sum_y,
    weight_ref,
    inv_ref,
    id_ref,
    by_ref,
    bxs_ref,
    bxr_ref,
    bzs_ref,
    bzr_ref,
    load_sem,
    send_sem,
    recv_sem,
):
    yn, xn, zn, cn = sizes
    gx, gy = lax.axis_index("gx"), lax.axis_index("gy")
    my, mx = gx // xn, gx % xn

    def to_y(d):
        return (((my + d) % yn) * xn + mx, gy)

    def to_x(d):
        return (my * xn + (mx + d) % xn, gy)

    across, along = yn * xn, zn * cn

    def to_gx(d):
        return ((gx + d) % across, gy)

    def to_gy(d):
        return (gx, (gy + d) % along)

    around = [
        ((gx + 1) % (yn * xn), gy),
        ((gx + yn * xn - 1) % (yn * xn), gy),
        (gx, (gy + 1) % (zn * cn)),
        (gx, (gy + zn * cn - 1) % (zn * cn)),
    ]
    axes = [(to_gx, across), (to_gy, along)]

    moved = [
        (count_hbm, count_ref),
        (owner_hbm, owner_ref),
        (node_hbm, node_ref),
        (val_hbm, val_ref),
        (param_hbm, param_ref),
        (mask_hbm, mask_ref),
        (edge_hbm, edge_ref),
        (diag_hbm, diag_ref),
        (surf_hbm, surf_ref),
        (box_hbm, box_ref),
    ]
    loads = [
        pltpu.make_async_copy(src, dst, load_sem.at[n]) for n, (src, dst) in enumerate(moved)
    ]
    for copy in loads:
        copy.start()

    barrier = pltpu.get_barrier_semaphore()
    greeted = 0
    for target, size in axes:
        for d in range(1, size):
            pl.semaphore_signal(
                barrier, inc=1, device_id=target(d), device_id_type=pl.DeviceIdType.MESH
            )
            greeted += 1

    used = [0]

    def send(src, dst, target):
        slot = used[0]
        used[0] += 1
        copy = pltpu.make_async_remote_copy(
            src_ref=src,
            dst_ref=dst,
            send_sem=send_sem.at[slot],
            recv_sem=recv_sem.at[slot],
            device_id=target,
            device_id_type=pl.DeviceIdType.MESH,
        )
        copy.start()
        return copy

    def finish(copies):
        for copy in copies:
            copy.wait()

    owners = across
    for copy in loads[:4]:
        copy.wait()
    nodes = node_ref[...]
    lines = [val_ref[0:1, :], val_ref[2:3, :], val_ref[1:2, :], nodes.astype(F32)]
    for n, line in enumerate(lines):
        high, low = halves(line)
        at = n % 2 + 4 * (n // 2)
        v8_ref[at : at + 1, :] = high.astype(F32)
        v8_ref[at + 2 : at + 3, :] = low.astype(F32)
    rows = nodes.shape[1]
    live = iota((1, rows), 1) < count_ref[...]
    owner = jnp.where(live, owner_ref[...], -1)
    upper = (iota((128, 128), 0) <= iota((128, 128), 1)).astype(BF16)
    before = jnp.zeros((owners, 1), F32)
    binned = jnp.zeros((owners * 8, 128), F32)
    for b in range(rows // 128):
        cut = slice(128 * b, 128 * b + 128)
        hot = (iota((owners, 128), 0) == owner[:, cut]).astype(F32)
        order = mm(hot.astype(BF16), upper) + before
        before = before + jnp.sum(hot, axis=1, keepdims=True)
        rank = jnp.sum(hot * order, axis=0, keepdims=True) - 1.0
        place = ((iota((128, 128), 0) & 63).astype(F32) == rank).astype(BF16)
        spread = (hot[:, None, :] * v8_ref[:, cut][None, :, :]).reshape(owners * 8, 128)
        binned = binned + mm(spread.astype(BF16), place, NT)
    binned = binned.reshape(owners, 8, 128)
    near = binned[:, 0:2, :] + binned[:, 2:4, :]
    far = binned[:, 4:6, :] + binned[:, 6:8, :]
    bin_ref[...] = jnp.where(iota((owners, 2, 128), 2) < 64, near, far)

    pl.semaphore_wait(barrier, greeted)
    copies = [
        send(bin_ref.at[(gx + d) % across], rx_ref.at[d], to_gx(d)) for d in far_first(across)
    ]
    rx_ref[0] = bin_ref[gx]

    loads[9].wait()
    tiles = surf_ref.shape[0]
    ids = box_ref[...].astype(F32)
    ids = jnp.concatenate([ids, jnp.zeros((1, 128 - tiles), F32)], axis=1)
    id_ref[0] = ids
    id_copies = [send(id_ref.at[0], id_ref.at[d], to_y(d)) for d in far_first(yn)]

    def bern(coord, index):
        other = 1.0 - coord
        return jnp.where(
            index == 0,
            other * other * other,
            jnp.where(
                index == 1,
                3.0 * coord * other * other,
                jnp.where(index == 2, 3.0 * coord * coord * other, coord * coord * coord),
            ),
        )

    line = iota((64, 128), 0)

    def weights(t, carry):
        cut = pl.ds(pl.multiple_of(t * 128, 128), 128)
        first = bern(param_ref[0:1, cut], line // 16)
        second = bern(param_ref[1:2, cut], (line // 4) % 4)
        third = bern(param_ref[2:3, cut], line % 4)
        weight_ref[t] = first * second * third
        return carry

    loads[4].wait()
    lax.fori_loop(0, tiles, weights, 0)

    for copy in loads[5:9]:
        copy.wait()
    for n in range(3):
        inv_ref[n] = 1.0 / diag_ref[4 * n]
    for d in range(4):
        keep = mask_ref[d].astype(F32)
        for n in range(9):
            edge_ref[d, n] = edge_ref[d, n] * keep

    finish(copies)
    left_half = iota((2, 128), 1) < 64

    def scatter(t, total):
        lefts, cols = [], []
        for k in range(4):
            one, two = rx_ref[8 * t + 2 * k], rx_ref[8 * t + 2 * k + 1]
            near = jnp.where(left_half, one, pltpu.roll(two, 64, 1))
            far = jnp.where(left_half, pltpu.roll(one, 64, 1), two)
            node = far[1:2, :].astype(jnp.int32)
            row_hot = iota((64, 128), 0) == (node >> 7)
            cols.append((iota((128, 128), 0) == (node & 127)).astype(BF16))
            values = [near[0:1, :], far[0:1, :], near[1:2, :]]
            left = jnp.concatenate([jnp.where(row_hot, v, 0.0) for v in values], axis=0)
            lefts.append(jnp.concatenate(halves(left), axis=0))
        return total + mm(jnp.concatenate(lefts, axis=1), jnp.concatenate(cols, axis=1), NT)

    load = lax.fori_loop(0, owners // 8, scatter, jnp.zeros((384, 128), F32))
    load = load[0:192] + load[192:384]
    comps = range(3)
    residual = [load[64 * c : 64 * c + 64] for c in comps]

    row_id, lane_id = iota((64, 128), 0), iota((64, 128), 1)
    same = row_id == lane_id
    zero_rows = jnp.zeros((5, 128), F32)

    def operator(field, h):
        def product(d, part=slice(0, 64)):
            return [
                edge_ref[d, c, part] * field[0][part]
                + edge_ref[d, 3 + c, part] * field[1][part]
                + edge_ref[d, 6 + c, part] * field[2][part]
                for c in comps
            ]

        def column(value, lane):
            wide = jnp.broadcast_to(value[:, lane : lane + 1], (64, 128))
            return jnp.sum(jnp.where(same, wide, 0.0), axis=0, keepdims=True)

        def give(k, lines):
            halo_s[h, k] = jnp.concatenate(lines + [zero_rows], axis=0)
            return send(halo_s.at[h, k], halo_r.at[h, k], around[k])

        copies = [
            give(0, [line[7:8, :] for line in product(0, slice(56, 64))]),
            give(1, [line[0:1, :] for line in product(1, slice(0, 8))]),
        ]
        up_y, low_y = product(2), product(3)
        copies.append(give(2, [column(up_y[c], 127) for c in comps]))
        copies.append(give(3, [column(low_y[c], 0) for c in comps]))
        up_x, low_x = product(0), product(1)
        inner = [
            sum(diag_ref[3 * k + c] * field[k] for k in comps if k != c)
            + jnp.where(row_id == 0, 0.0, pltpu.roll(up_x[c], 1, 0))
            + jnp.where(row_id == 63, 0.0, pltpu.roll(low_x[c], 63, 0))
            + jnp.where(lane_id == 0, 0.0, pltpu.roll(up_y[c], 1, 1))
            + jnp.where(lane_id == 127, 0.0, pltpu.roll(low_y[c], 127, 1))
            for c in comps
        ]
        finish(copies)
        there = [gx > 0, gx < yn * xn - 1, gy > 0, gy < zn * cn - 1]
        got = [halo_r[h, k] * there[k].astype(F32) for k in range(4)]

        def upright(row):
            wide = jnp.broadcast_to(row, (64, 128))
            return jnp.sum(jnp.where(same, wide, 0.0), axis=1, keepdims=True)

        return [
            inner[c]
            + jnp.where(row_id == 0, got[0][c : c + 1, :], 0.0)
            + jnp.where(row_id == 63, got[1][c : c + 1, :], 0.0)
            + jnp.where(lane_id == 0, upright(got[2][c : c + 1, :]), 0.0)
            + jnp.where(lane_id == 127, upright(got[3][c : c + 1, :]), 0.0)
            for c in comps
        ]

    def partial(a, b):
        return jnp.sum(a[0] * b[0] + a[1] * b[1] + a[2] * b[2], axis=0, keepdims=True)

    search = [residual[c] * inv_ref[c] for c in comps]
    other = operator(search, 0)
    second = [other[c] * inv_ref[c] for c in comps]
    third = operator(second, 1)
    lines = [
        partial(search, residual),
        partial(search, other),
        partial(second, other),
        partial(search, third),
        partial(second, third),
    ]
    total = jnp.concatenate(lines + [jnp.zeros((8 - len(lines), 128), F32)], axis=0)
    for shift in (64, 32, 16):
        total = total + pltpu.roll(total, shift, 1)
    group = iota((8, 128), 1) // 16 == iota((8, 128), 0)
    total = jnp.sum(jnp.where(group, total, 0.0), axis=0, keepdims=True)

    pieces = halves(jnp.concatenate(search, axis=0)) + halves(jnp.concatenate(second, axis=0))
    stacked = jnp.concatenate(pieces, axis=0)

    def term(t, terms):
        nodes = [surf_ref[pl.ds(2 * t + k, 1), :] for k in range(2)]
        cols = [(iota((128, 128), 0) == (node & 127)).astype(BF16) for node in nodes]
        picked = mm(stacked, jnp.concatenate(cols, axis=1))
        tops, bottoms, heres = [], [], []
        for k in range(2):
            row_hot = iota((64, 128), 0) == (nodes[k] >> 7)
            weight = weight_ref[2 * t + k]
            parts = []
            for first in (0, 384):
                for c in comps:
                    at = first + 64 * c
                    side = picked[:, 128 * k : 128 * k + 128]
                    both = side[at : at + 64] + side[at + 192 : at + 256]
                    value = jnp.sum(jnp.where(row_hot, both, 0.0), axis=0, keepdims=True)
                    parts.append(weight * value)
            high, low = halves(jnp.concatenate(parts, axis=0))
            tops.append(high)
            bottoms.append(low)
            heres.append((iota((tiles, 128), 0) == 2 * t + k).astype(BF16))
        here = jnp.concatenate(heres, axis=1)
        high, low = jnp.concatenate(tops, axis=1), jnp.concatenate(bottoms, axis=1)
        return terms + mm(here, high, NT) + mm(here, low, NT)

    half = tiles // 2
    per_y, per_x = xn * along, along

    def box_picks():
        finish(id_copies)
        own = id_ref[0]
        lane = iota((1, 128), 1)
        id_all, id_low = own, jnp.where(lane < half, own, 0.0)
        id_high = pltpu.roll(jnp.where(lane < half, 0.0, own), 128 - half, 1)
        for d in range(1, yn):
            line = id_ref[d]
            id_all = id_all + pltpu.roll(line, tiles * d, 1)
            id_low = id_low + pltpu.roll(jnp.where(lane < half, line, 0.0), half * d, 1)
            turned = jnp.where(lane < half, 0.0, line)
            id_high = id_high + pltpu.roll(turned, (128 + half * (d - 1)) % 128, 1)

        def chosen(ids, width):
            wanted = (my * per_y + iota((per_y, 128), 0)).astype(F32)
            return (wanted == ids).astype(F32)[:, :width].astype(BF16)

        return (
            chosen(id_all, yn * tiles),
            chosen(id_low, yn * half),
            chosen(id_high, yn * half),
        )

    terms = jnp.zeros((tiles, 384), F32)
    ends = [0, 5 * tiles // 16, tiles // 2]
    for stage, landing in enumerate((sum_x, sum_y)):
        target, size = axes[stage]
        sum_s[stage] = total
        copies = [send(sum_s.at[stage], landing.at[d - 1], target(d)) for d in far_first(size)]
        if stage == 1:
            pick_all, pick_low, pick_high = box_picks()
        terms = lax.fori_loop(ends[stage], ends[stage + 1], term, terms)
        finish(copies)
        for d in range(1, size):
            total = total + landing[d - 1]
    total = jnp.where(group, jnp.broadcast_to(total, (8, 128)), 0.0)
    total = jnp.sum(total, axis=1, keepdims=True)
    norm, bend_a, bend_b, bend_c, bend_d = [total[q : q + 1, :] for q in range(5)]

    whole = norm + bend_a
    step = norm / whole
    rest = bend_a / whole
    norm_next = (norm / whole) * ((norm * bend_b - bend_a * bend_a) / whole)
    turn = norm_next / norm
    front = rest + turn
    bend_next = (
        front * front * whole
        - front * step * (2.0 * bend_a + bend_c + bend_b)
        + step * step * (bend_b + bend_d)
    )
    step_next = norm_next / bend_next
    alpha = step + step_next * front
    gamma = step * step_next

    terms = alpha * terms[:, 0:192] - gamma * terms[:, 192:384]
    by_ref[0, 0:tiles, :] = terms[:, 0:128]
    by_ref[0, tiles:, :] = jnp.concatenate([terms[:half, 128:192], terms[half:, 128:192]], axis=1)
    copies = [send(by_ref.at[0], by_ref.at[d], to_y(d)) for d in far_first(yn)]
    for c in comps:
        field_ref[c] = alpha * search[c] - gamma * second[c]
    finish(copies)
    high, low = halves(by_ref[:, 0:tiles, :].reshape(yn * tiles, 128))
    dense = mm(pick_all, high) + mm(pick_all, low)
    high, low = halves(by_ref[:, tiles:, :].reshape(yn * half, 128))
    near = mm(pick_low, high) + mm(pick_low, low)
    far = mm(pick_high, high) + mm(pick_high, low)
    near = jnp.where(iota(near.shape, 1) < 64, near + pltpu.roll(far, 64, 1), 0.0)
    dense = jnp.concatenate([dense, near], axis=1)
    bxs_ref[...] = dense.reshape(xn, per_x, 256)
    copies = [send(bxs_ref.at[(mx + d) % xn], bxr_ref.at[d - 1], to_x(d)) for d in far_first(xn)]
    dense = bxs_ref[mx]
    finish(copies)
    for d in range(1, xn):
        dense = dense + bxr_ref[d - 1]
    for k in range(along):
        bzs_ref[k] = dense[k : k + 1, :]
    copies = [
        send(bzs_ref.at[(gy + d) % along], bzr_ref.at[d - 1], to_gy(d)) for d in far_first(along)
    ]
    dense = bzs_ref[gy]
    finish(copies)
    for d in range(1, along):
        dense = dense + bzr_ref[d - 1]
    grad_ref[...] = dense[:, 0:192]


def per_device(
    sizes,
    diag_blocks,
    edge_blocks,
    edge_mask,
    src_values,
    src_owner,
    src_node,
    src_count,
    surf_node,
    surf_param,
    tile_box,
):
    yn, xn, zn, cn = sizes
    tiles = tile_box.shape[0]
    rows = src_node.shape[0]
    vmem = pl.BlockSpec(memory_space=pltpu.VMEM)
    across, per_x = yn * xn, zn * cn
    copies = 2 * (across - 1) + 2 * (per_x - 1) + 2 * (yn - 1) + xn - 1 + 8

    def buf(*shape):
        return pltpu.VMEM(shape, F32)

    operands = (
        src_count.reshape(1, 1),
        tile_box.reshape(1, tiles),
        diag_blocks,
        edge_blocks,
        edge_mask,
        src_values,
        src_owner.reshape(1, rows),
        src_node.reshape(1, rows),
        surf_node.reshape(tiles, 128),
        surf_param,
    )
    return pl.pallas_call(
        functools.partial(kernel, sizes),
        out_shape=(
            jax.ShapeDtypeStruct((3,) + diag_blocks.shape[1:], F32),
            jax.ShapeDtypeStruct((1, 192), F32),
        ),
        in_specs=[pl.BlockSpec(memory_space=pl.ANY)] * len(operands),
        out_specs=(vmem, vmem),
        scratch_shapes=[pltpu.VMEM(x.shape, x.dtype) for x in operands]
        + [
            buf(8, rows),
            buf(across, 2, 128),
            buf(across, 2, 128),
            buf(2, 4, 8, 128),
            buf(2, 4, 8, 128),
            buf(2, 1, 128),
            buf(across - 1, 1, 128),
            buf(per_x - 1, 1, 128),
            buf(tiles, 64, 128),
            buf(3, 64, 128),
            buf(yn, 1, 128),
            buf(yn, tiles * 3 // 2, 128),
            buf(xn, per_x, 256),
            buf(xn - 1, per_x, 256),
            buf(per_x, 1, 256),
            buf(per_x - 1, 1, 256),
            pltpu.SemaphoreType.DMA((len(operands),)),
            pltpu.SemaphoreType.DMA((copies,)),
            pltpu.SemaphoreType.DMA((copies,)),
        ],
        compiler_params=pltpu.CompilerParams(
            collective_id=0, has_side_effects=True, vmem_limit_bytes=60 * 2**20
        ),
    )(*operands)


def solution(mesh):
    across, along = mesh.shape["gx"], mesh.shape["gy"]
    xn = 4 if across >= 16 else 2
    sizes = (across // xn, xn, along // 2, 2)
    return jax.shard_map(
        functools.partial(per_device, sizes),
        mesh=mesh,
        in_specs=(
            P(None, "gx", "gy"),
            P(None, None, "gx", "gy"),
            P(None, "gx", "gy"),
            P(None, ("gx", "gy")),
            P(("gx", "gy"), None),
            P(("gx", "gy")),
            P(("gx", "gy")),
            P(("gx", "gy")),
            P(None, ("gx", "gy")),
            P(("gx", "gy")),
        ),
        out_specs=(P(None, "gx", "gy"), P(("gx", "gy"), None)),
        check_vma=False,
    )
```
